256 devices in a mesh: head: 8 (over x, core), blk: 32 (over y, z).
Axes of the slice: x: 4, y: 4, z: 8, core: 2. Of those that a mesh axis runs over, the one named last changes fastest.
Arguments:
- hidden_in: bfloat16 [512, 2048], P('blk', 'head'), may hold values from -6 to 6
- qkv_weight: bfloat16 [2048, 3, 2048], P(None, None, 'head'), may hold values from -0.125 to 0.125
- out_weight: bfloat16 [2048, 2048], P('head'), may hold values from -0.125 to 0.125
- cache_pool: bfloat16 [2048, 64, 2, 2048], P('blk', None, None, 'head'), may hold values from -6 to 6
- page_table: int32 [512, 4], P('blk'), may hold values from 0 to 63, as said below
- request_order: int32 [512], replicated, may hold values from 0 to 511, as said below
- request_lengths: int32 [512], replicated, may hold values from 128 to 256, as said below
- retained_counts: int32 [512], replicated, may hold values from 32 to 128, as said below
- retained_positions: int32 [512, 128], replicated, may hold values from 0 to 255, as said below
- blended_weight: float32 [512, 256], replicated, may hold values from 0.05 to 1
Outputs:
- hidden_out: bfloat16 [512, 2048], P('blk', 'head')
- packed_cache: bfloat16 [512, 132, 2, 2048], P('blk', None, None, 'head')
The draws below stay inside these ranges and needn't reach their ends.
Inputs may be any that keep to these rules, and one draw needn't show every extreme that they name: `request_order`: a permutation of all 512 positions; of the 16 old positions of one blk index (b * 16 to b * 16 + 15), at most 1 stand at new positions of any one blk index, and exactly 1 at those of some index; the requests at new blk index c come from 16 old blk indices c - k (counted round, k distinct), among which k = 1 and k = 16 always. `page_table`: row r names pool rows counted from the first pool row of blk index r // 16; the 64 pool rows of an index are each named once. `request_lengths`: some request has 256. `retained_counts`: between request_lengths[r] // 4 and request_lengths[r] // 2; some request keeps 128. `retained_positions`: the first retained_counts[r] entries of row r are distinct positions below request_lengths[r], rising; the others are 0.
All inputs are finite; a program needn't handle non-finite values.
Results may differ from the reference program's by a relative error of at most 0.02.
Values may be sent and summed in bfloat16 or wider, within the bound.
No kernel may reach another device: no remote copies, remote signals or barrier semaphores. Data moves between devices by JAX's collectives and lax.ppermute only.
A program may use at most 128 MiB of HBM per device.

```python
import math
import jax
import jax.numpy as jnp
from jax import lax

D = 2048
HEADS = 16
HEAD_DIM = 128
REQ_BLK = 16
PAGE = 64
PAGES = 4
REQS = 512
CAP = 256
KEPT = 128
SLOTS = 132
CAPACITY = 1


def keep_plan(key):
    base = jax.random.fold_in(key, 7)
    key_len, key_count, key_score, key_top = jax.random.split(base, 4)
    length_values = jax.random.randint(key_len, (REQS,), CAP // 2, CAP + 1, dtype=jnp.int32)
    longest = jax.random.randint(key_top, (), 0, REQS, dtype=jnp.int32)
    length_values = length_values.at[longest].set(CAP)
    count_values = jax.random.randint(key_count, (REQS,), length_values // 4, length_values // 2 + 1, dtype=jnp.int32)
    count_values = count_values.at[longest].set(CAP // 2)
    positions = jnp.arange(CAP, dtype=jnp.int32)
    scores = jax.random.randint(key_score, (REQS, CAP), 0, 2 ** 20, dtype=jnp.int32) * CAP + positions[None, :]
    scores = jnp.where(positions[None, :] < length_values[:, None], scores, scores + 2 ** 20 * CAP)
    ordering = jnp.argsort(scores, axis=1)
    rank_of = jnp.argsort(ordering, axis=1)
    chosen = rank_of < count_values[:, None]
    ordered = jnp.argsort(jnp.where(chosen, positions[None, :], CAP + positions[None, :]), axis=1)[:, :KEPT].astype(jnp.int32)
    slot_index = jnp.arange(KEPT, dtype=jnp.int32)
    keep_rows = jnp.where(slot_index[None, :] < count_values[:, None], ordered, 0)
    return (length_values, count_values, keep_rows)


def draw_request_lengths(key, part):
    return keep_plan(key)[0]


def draw_retained_counts(key, part):
    return keep_plan(key)[1]


def draw_retained_positions(key, part):
    return keep_plan(key)[2]


def local_orders(key, devices_count, length):

    def shuffle(subkey):
        return jax.random.permutation(subkey, length)
    return jax.vmap(shuffle)(jax.random.split(key, devices_count))


def draw_request_order(key, part):
    base = jax.random.fold_in(key, 11)
    key_shift, key_source, key_slot = jax.random.split(base, 3)
    devices_count = REQS // REQ_BLK
    groups = REQ_BLK // CAPACITY
    shift_index = jnp.arange(devices_count, dtype=jnp.int32)
    shift_scores = jax.random.randint(key_shift, (devices_count,), 0, 2 ** 16, dtype=jnp.int32) * devices_count + shift_index
    shift_scores = jnp.where(shift_index == 1, -2, shift_scores)
    shift_scores = jnp.where(shift_index == devices_count // 2, -1, shift_scores)
    shift_values = jnp.argsort(shift_scores, stable=True)[:groups].astype(jnp.int32)
    shifts = jnp.repeat(shift_values, CAPACITY)
    source_order = local_orders(key_source, devices_count, REQ_BLK)
    slot_order = local_orders(key_slot, devices_count, REQ_BLK)
    targets = jnp.arange(devices_count, dtype=jnp.int32)[:, None]
    sources = (targets - shifts[None, :]) % devices_count
    old_ids = sources * REQ_BLK + source_order[sources, jnp.arange(REQ_BLK, dtype=jnp.int32)[None, :]]
    new_ids = targets * REQ_BLK + slot_order
    return jnp.zeros((REQS,), jnp.int32).at[new_ids.reshape(-1)].set(old_ids.reshape(-1).astype(jnp.int32))


def draw_page_table(key, part):
    base = jax.random.fold_in(key, 13)
    devices_count = REQS // REQ_BLK
    pool_orders = local_orders(base, devices_count, REQ_BLK * PAGES)
    return pool_orders.reshape(REQS, PAGES).astype(jnp.int32)


def shard_levels(rng, extent, cuts, low, largest):
    factor_of = 1.0
    for position, shards_of in cuts:
        steps = jax.random.uniform(jax.random.fold_in(jax.random.fold_in(rng, 6), position), (shards_of,), jnp.float32, low / len(cuts), largest / len(cuts))
        factor_of = factor_of * jnp.repeat(jnp.exp(steps), extent[position] // shards_of).reshape((-1,) + (1,) * (len(extent) - 1 - position))
    return factor_of


def centred(own_key, dims, deviation, bound, shards=(), kind=jnp.bfloat16):
    array = jax.random.normal(own_key, dims, jnp.float32) * deviation
    if len(shards) > 0:
        array = shard_levels(own_key, dims, shards, -0.22, 0.18) * array
    return jnp.clip(array, min=-bound, max=bound).astype(kind)


def setup_inputs(seed: int = 0) -> dict:
    keys = jax.random.split(jax.random.key(seed), 11)
    return {
        "hidden_in": centred(keys[0], (REQS, D), 1.0, 6.0, ((0, 32), (1, 8))),
        "qkv_weight": centred(keys[1], (D, 3, D), D ** -0.5, 0.125, ((2, 8),)),
        "out_weight": centred(keys[2], (D, D), D ** -0.5, 0.125, ((0, 8),)),
        "cache_pool": centred(keys[3], (REQS * PAGES, PAGE, 2, D), 1.0, 6.0, ((0, 32), (3, 8))),
        "page_table": draw_page_table(jax.random.fold_in(keys[10], 71), 0),
        "request_order": draw_request_order(jax.random.fold_in(keys[10], 71), 0),
        "request_lengths": draw_request_lengths(jax.random.fold_in(keys[10], 71), 0),
        "retained_counts": draw_retained_counts(jax.random.fold_in(keys[10], 71), 0),
        "retained_positions": draw_retained_positions(jax.random.fold_in(keys[10], 71), 0),
        "blended_weight": jnp.clip(jnp.exp(jax.random.uniform(keys[9], (REQS, CAP), jnp.float32, math.log(0.05), math.log(1.0))), 0.05, 1.0),
    }


epsilon = 1e-05

def layer_norm(hidden):
    average = lax.optimization_barrier(jnp.mean(hidden, axis=-1, keepdims=True))
    centered = hidden - average
    variance = lax.optimization_barrier(jnp.mean(centered * centered, axis=-1, keepdims=True))
    return centered * lax.rsqrt(variance + epsilon)

def rotate(vectors, positions):
    half_dim = vectors.shape[-1] // 2
    inverse_freq = 10000.0 ** (-jnp.arange(half_dim, dtype=jnp.float32) / half_dim)
    angles = positions.astype(jnp.float32)[:, None, None] * inverse_freq
    cosine = jnp.cos(angles)
    sine_part = jnp.sin(angles)
    first_half = vectors[..., :half_dim]
    second_half = vectors[..., half_dim:]
    return jnp.concatenate([first_half * cosine - second_half * sine_part, second_half * cosine + first_half * sine_part], axis=-1)

def packing_layout(retain_flags, count_values, length_values, weight_factors):
    kept_total = retain_flags.shape[1]
    capacity_rows = weight_factors.shape[1]
    page_total = capacity_rows // PAGE
    slot_index = jnp.arange(kept_total, dtype=jnp.int32)
    slot_active = slot_index[None, :] < count_values[:, None]
    positions = jnp.arange(capacity_rows, dtype=jnp.int32)
    matches = (retain_flags[:, :, None] == positions[None, None, :]) & slot_active[:, :, None]
    dropped = (positions[None, :] < length_values[:, None]) & jnp.logical_not(jnp.any(matches, axis=1))
    dropped_weight = jnp.where(dropped, weight_factors, jnp.zeros((), weight_factors.dtype))
    page_match = (positions // PAGE)[None, :] == jnp.arange(page_total, dtype=jnp.int32)[:, None]
    spread = jnp.where(page_match[None], dropped_weight[:, None, :], jnp.zeros((), weight_factors.dtype))
    blending_factors = spread.astype(jnp.bfloat16)
    dropped_mass = jnp.log(1.0 + lax.optimization_barrier(jnp.sum(spread, axis=2)))
    page_live = (jnp.arange(page_total, dtype=jnp.int32) * PAGE)[None, :] < length_values[:, None]
    valid_flags = jnp.concatenate([slot_active, page_live], axis=1)
    logit_bias = jnp.concatenate([jnp.zeros((retain_flags.shape[0], kept_total), weight_factors.dtype), dropped_mass], axis=1)
    return (blending_factors, logit_bias, valid_flags, slot_active)

def attend(queries, new_key, new_value, packed, logit_bias, valid_flags):
    heads_count = queries.shape[0]
    head_size = queries.shape[1]
    head_width = heads_count * head_size
    score_scale = head_size ** (-0.5)
    key_rows = packed[:, :head_width].astype(jnp.float32).reshape(-1, heads_count, head_size)
    value_rows = packed[:, head_width:].astype(jnp.float32).reshape(-1, heads_count, head_size)
    query_wide = queries.astype(jnp.float32)
    scores = jnp.einsum('hd,shd->hs', query_wide, key_rows, precision=lax.Precision.HIGHEST) * score_scale + logit_bias[None, :]
    scores = jnp.where(valid_flags[None, :], scores, -1e+30)
    own_score = lax.optimization_barrier(jnp.sum(query_wide * new_key.astype(jnp.float32), axis=-1)) * score_scale
    highest = jnp.maximum(lax.optimization_barrier(jnp.max(scores, axis=-1)), own_score)
    exponentials = jnp.exp(scores - highest[:, None])
    own_exp = jnp.exp(own_score - highest)
    denominator = lax.optimization_barrier(jnp.sum(exponentials, axis=-1)) + own_exp
    probabilities = (exponentials / denominator[:, None]).astype(jnp.bfloat16)
    own_prob = (own_exp / denominator).astype(jnp.bfloat16)
    combined = jnp.einsum('hs,shd->hd', probabilities.astype(jnp.float32), value_rows, precision=lax.Precision.HIGHEST)
    combined = combined + own_prob.astype(jnp.float32)[:, None] * new_value.astype(jnp.float32)
    return combined.astype(jnp.bfloat16).reshape(head_width)

def reference(hidden_in, qkv_weight, out_weight, cache_pool, page_table, request_order, request_lengths, retained_counts, retained_positions, blended_weight):
    hidden = hidden_in.astype(jnp.float32)
    normed = layer_norm(hidden).astype(jnp.bfloat16)
    projections = jnp.dot(normed, qkv_weight.reshape(D, 3 * D), preferred_element_type=jnp.float32).reshape(REQS, 3, HEADS, HEAD_DIM)
    old_ids = request_order
    positions = request_lengths[old_ids]
    queries = rotate(projections[:, 0], positions).astype(jnp.bfloat16)
    new_keys = rotate(projections[:, 1], positions).astype(jnp.bfloat16)
    new_values = projections[:, 2].astype(jnp.bfloat16)
    blending_factors, logit_bias, valid_flags, slot_active = packing_layout(retained_positions, retained_counts, request_lengths, blended_weight)

    def per_request(request_item):
        request, query_row, key_row, value_row = request_item
        page_rows = request // REQ_BLK * (REQ_BLK * PAGES) + page_table[request]
        cache_rows = cache_pool[page_rows].reshape(CAP, 2 * D)
        kept_rows = jnp.where(slot_active[request][:, None], cache_rows[retained_positions[request]], jnp.zeros((), jnp.bfloat16))
        merged_rows = jnp.dot(blending_factors[request], cache_rows, preferred_element_type=jnp.float32).astype(jnp.bfloat16)
        packed = jnp.concatenate([kept_rows, merged_rows], axis=0)
        attended = attend(query_row, key_row, value_row, packed, logit_bias[request], valid_flags[request])
        return (attended, packed.reshape(SLOTS, 2, D))
    attended, packed_cache = lax.map(per_request, (old_ids, queries, new_keys, new_values))
    projected = jnp.dot(attended, out_weight, preferred_element_type=jnp.float32)
    hidden_out = (hidden + projected).astype(jnp.bfloat16)
    return (hidden_out, packed_cache)
```

```python
import jax
import jax.numpy as jnp
from jax import lax
from jax.experimental import pallas as pl
from jax.experimental.pallas import tpu as pltpu
from jax.sharding import PartitionSpec as P

HEAD_DIM = 128
PAGE = 64
PAGES = 4
CAP = 256
KEPT = 128
SLOTS = 132
HEADS_HERE = 2
LANES = HEADS_HERE * 2
ROWS = SLOTS * LANES
PAD_ROWS = 640
NEG = -1e30

epsilon = 1e-05


def layer_norm(hidden):
    average = jnp.mean(hidden, axis=-1, keepdims=True)
    centered = hidden - average
    variance = jnp.mean(centered * centered, axis=-1, keepdims=True)
    return centered * lax.rsqrt(variance + epsilon)


def rotate(vectors, positions):
    half_dim = vectors.shape[-1] // 2
    inverse_freq = 10000.0 ** (-jnp.arange(half_dim, dtype=jnp.float32) / half_dim)
    angles = positions.astype(jnp.float32)[:, None, None] * inverse_freq
    cosine = jnp.cos(angles)
    sine_part = jnp.sin(angles)
    first_half = vectors[..., :half_dim]
    second_half = vectors[..., half_dim:]
    return jnp.concatenate(
        [
            first_half * cosine - second_half * sine_part,
            second_half * cosine + first_half * sine_part,
        ],
        axis=-1,
    )


def pack_kernel(
    target_ref,
    page_ref,
    keep_smem,
    keep_ref,
    length_ref,
    weight_ref,
    cache_rows_hbm,
    cache_flat_hbm,
    send_hbm,
    rows_vmem,
    flat_vmem,
    out_vmem,
    wide_vmem,
    in_sem,
    flat_sem,
    out_sem,
):
    count = keep_ref.shape[0]

    def page_copies(i):
        copies = []
        for j in range(PAGES):
            page = page_ref[j, i]
            copies.append(
                pltpu.make_async_copy(
                    cache_rows_hbm.at[page],
                    rows_vmem.at[i, pl.ds(j * PAGE, PAGE)],
                    in_sem.at[i, j],
                )
            )
            copies.append(
                pltpu.make_async_copy(
                    cache_flat_hbm.at[page],
                    flat_vmem.at[i, pl.ds(j * PAGE * LANES, PAGE * LANES)],
                    flat_sem.at[i, j],
                )
            )
        return copies

    def start(i, carry):
        for copy in page_copies(i):
            copy.start()
        return carry

    lax.fori_loop(0, count, start, 0)

    keep_cols = jnp.transpose(keep_ref[...].astype(jnp.float32))
    lane_pos = lax.broadcasted_iota(jnp.int32, (KEPT, CAP), 1).astype(jnp.float32)
    kept_rows = []
    for i in range(count):
        match = keep_cols[:, i : i + 1] == lane_pos
        kept_rows.append(jnp.max(jnp.where(match, 1.0, 0.0), axis=0, keepdims=True))
    kept = jnp.concatenate(kept_rows, axis=0)
    spots = lax.broadcasted_iota(jnp.int32, (count, CAP), 1)
    dropped = (spots < length_ref[...]) & (kept < 0.5)
    factors = jnp.where(dropped, weight_ref[...], 0.0).astype(jnp.bfloat16)
    spread = (
        lax.broadcasted_iota(jnp.int32, (CAP, CAP * LANES), 1) // LANES
        == lax.broadcasted_iota(jnp.int32, (CAP, CAP * LANES), 0)
    )
    spread = jnp.where(spread, 1.0, 0.0).astype(jnp.bfloat16)
    wide_vmem[...] = jnp.dot(factors, spread, preferred_element_type=jnp.float32)
    row_id = lax.broadcasted_iota(jnp.int32, (PAGES * LANES, CAP * LANES), 0)
    lane_id = lax.broadcasted_iota(jnp.int32, (PAGES * LANES, CAP * LANES), 1)
    selector = (row_id // LANES == lane_id // (PAGE * LANES)) & (row_id % LANES == lane_id % LANES)
    selector = jnp.where(selector, 1.0, 0.0)
    zero_row = jnp.zeros((1, LANES, HEAD_DIM), jnp.bfloat16)

    def out_copy(i):
        return pltpu.make_async_copy(out_vmem.at[i], send_hbm.at[target_ref[i]], out_sem.at[i])

    def body(i, carry):
        for copy in page_copies(i):
            copy.wait()
        rows_vmem[i, pl.ds(CAP, 1)] = zero_row
        left = (selector * wide_vmem[pl.ds(i, 1), :]).astype(jnp.bfloat16)
        merged = jnp.dot(left, flat_vmem[i], preferred_element_type=jnp.float32)
        out_vmem[i, pl.ds(KEPT, PAGES)] = merged.astype(jnp.bfloat16).reshape(
            PAGES, LANES, HEAD_DIM
        )

        def chunk(c, inner):
            for u in range(16):
                s = c * 16 + u
                out_vmem[i, s] = rows_vmem[i, keep_smem[i, s]]
            return inner

        lax.fori_loop(0, KEPT // 16, chunk, 0)
        out_copy(i).start()
        return carry

    lax.fori_loop(0, count, body, 0)

    def finish(i, carry):
        out_copy(i).wait()
        return carry

    lax.fori_loop(0, count, finish, 0)


def pack(targets, pages, keep, lengths, weights, cache_pool, buffers):
    count = keep.shape[0]
    pool = cache_pool.shape[0]
    view = cache_pool.reshape(pool, PAGE, 2, HEADS_HERE, HEAD_DIM).transpose(0, 1, 3, 2, 4)
    as_rows = view.reshape(pool, PAGE, LANES, HEAD_DIM)
    as_flat = view.reshape(pool, PAGE * LANES, HEAD_DIM)
    whole = lambda: pl.BlockSpec(memory_space=pltpu.VMEM)
    hbm = lambda: pl.BlockSpec(memory_space=pl.ANY)
    return pl.pallas_call(
        pack_kernel,
        out_shape=jax.ShapeDtypeStruct((buffers, SLOTS, LANES, HEAD_DIM), jnp.bfloat16),
        grid_spec=pltpu.PrefetchScalarGridSpec(
            num_scalar_prefetch=3,
            grid=(),
            in_specs=[whole(), whole(), whole(), hbm(), hbm()],
            out_specs=hbm(),
            scratch_shapes=[
                pltpu.VMEM((count, CAP + 1, LANES, HEAD_DIM), jnp.bfloat16),
                pltpu.VMEM((count, CAP * LANES, HEAD_DIM), jnp.bfloat16),
                pltpu.VMEM((count, SLOTS, LANES, HEAD_DIM), jnp.bfloat16),
                pltpu.VMEM((count, CAP * LANES), jnp.float32),
                pltpu.SemaphoreType.DMA((count, PAGES)),
                pltpu.SemaphoreType.DMA((count, PAGES)),
                pltpu.SemaphoreType.DMA((count,)),
            ],
        ),
        compiler_params=pltpu.CompilerParams(vmem_limit_bytes=40 * 1024 * 1024),
        name="pack",
    )(targets, pages, keep, keep, lengths, weights, as_rows, as_flat)


def attend_kernel(
    source_ref,
    query_ref,
    key_ref,
    value_ref,
    bias_ref,
    weight_ref,
    recv_hbm,
    packed_hbm,
    share_ref,
    rows_vmem,
    attended_vmem,
    in_sem,
    out_sem,
):
    count = query_ref.shape[0]

    def in_copy(r):
        return pltpu.make_async_copy(
            recv_hbm.at[source_ref[r]], rows_vmem.at[r, pl.ds(0, ROWS)], in_sem.at[r]
        )

    def out_copy(r):
        return pltpu.make_async_copy(
            rows_vmem.at[r, pl.ds(0, ROWS)], packed_hbm.at[r], out_sem.at[r]
        )

    for r in range(count):
        in_copy(r).start()
    for r in range(count):
        rows_vmem[r, pl.ds(ROWS, PAD_ROWS - ROWS)] = jnp.zeros(
            (PAD_ROWS - ROWS, HEAD_DIM), jnp.bfloat16
        )
    scale = HEAD_DIM ** (-0.5)
    contract_last = (((1,), (1,)), ((), ()))
    own = (
        jnp.sum(
            query_ref[...].astype(jnp.float32) * key_ref[...].astype(jnp.float32),
            axis=-1,
            keepdims=True,
        )
        * scale
    )
    for r in range(count):
        in_copy(r).wait()
        out_copy(r).start()
        scores = lax.dot_general(
            query_ref[r], rows_vmem[r], contract_last, preferred_element_type=jnp.float32
        )
        scores = scores * scale + bias_ref[r]
        own_score = own[r]
        highest = jnp.maximum(jnp.max(scores, axis=-1, keepdims=True), own_score)
        exponentials = jnp.exp(scores - highest)
        own_exp = jnp.exp(own_score - highest)
        denominator = jnp.sum(exponentials, axis=-1, keepdims=True) + own_exp
        probabilities = exponentials / denominator
        own_prob = (own_exp / denominator).astype(jnp.bfloat16).astype(jnp.float32)
        moved = pltpu.roll(probabilities, 1, axis=1).astype(jnp.bfloat16)
        combined = jnp.dot(moved, rows_vmem[r], preferred_element_type=jnp.float32)
        combined = combined + own_prob * value_ref[r].astype(jnp.float32)
        attended_vmem[r] = combined
    attended = jnp.concatenate(
        [attended_vmem[:, h, :] for h in range(HEADS_HERE)], axis=1
    ).astype(jnp.bfloat16)
    share = jnp.dot(attended, weight_ref[...], preferred_element_type=jnp.float32).astype(
        jnp.bfloat16
    )
    peers = share_ref.shape[0]
    width = share_ref.shape[2]
    for e in range(peers):
        share_ref[e] = share[:, e * width : (e + 1) * width]
    for r in range(count):
        out_copy(r).wait()


def attend(sources, queries, keys, values, bias, out_weight, recv, peers):
    count = queries.shape[0]
    width = out_weight.shape[1] // peers
    whole = lambda: pl.BlockSpec(memory_space=pltpu.VMEM)
    hbm = lambda: pl.BlockSpec(memory_space=pl.ANY)
    return pl.pallas_call(
        attend_kernel,
        out_shape=(
            jax.ShapeDtypeStruct((count, ROWS, HEAD_DIM), jnp.bfloat16),
            jax.ShapeDtypeStruct((peers, count, width), jnp.bfloat16),
        ),
        grid_spec=pltpu.PrefetchScalarGridSpec(
            num_scalar_prefetch=1,
            grid=(),
            in_specs=[whole(), whole(), whole(), whole(), whole(), hbm()],
            out_specs=[hbm(), whole()],
            scratch_shapes=[
                pltpu.VMEM((count, PAD_ROWS, HEAD_DIM), jnp.bfloat16),
                pltpu.VMEM((count, 8, HEAD_DIM), jnp.float32),
                pltpu.SemaphoreType.DMA((count,)),
                pltpu.SemaphoreType.DMA((count,)),
            ],
        ),
        compiler_params=pltpu.CompilerParams(vmem_limit_bytes=32 * 1024 * 1024),
        name="attend",
    )(sources, queries, keys, values, bias, out_weight, recv)


def local(
    hidden_in,
    qkv_weight,
    out_weight,
    cache_pool,
    page_table,
    request_order,
    request_lengths,
    retained_counts,
    retained_positions,
    blended_weight,
):
    rows_here = hidden_in.shape[0]
    head_width = qkv_weight.shape[2]
    heads_here = head_width // HEAD_DIM
    blocks = lax.axis_size("blk")
    peers = lax.axis_size("head")
    block_index = lax.axis_index("blk")
    first = block_index * rows_here
    local_slots = jnp.arange(rows_here, dtype=jnp.int32)
    slot_index = jnp.arange(KEPT, dtype=jnp.int32)
    own_ids = first + local_slots

    places = jnp.arange(request_order.shape[0], dtype=jnp.int32) // rows_here
    targets = jnp.sum(
        jnp.where(request_order[None, :] == own_ids[:, None], places[None, :], 0), axis=1
    )
    take = lambda array: lax.dynamic_slice_in_dim(array, first, rows_here, 0)
    own_counts = take(retained_counts)
    own_keep = jnp.where(
        slot_index[None, :] < own_counts[:, None], take(retained_positions), CAP
    )
    outgoing = pack(
        targets,
        page_table.T,
        own_keep,
        take(request_lengths)[:, None],
        take(blended_weight),
        cache_pool,
        blocks,
    )
    outgoing = outgoing.reshape(blocks, ROWS, HEAD_DIM)
    arrived = lax.all_to_all(outgoing, "blk", split_axis=0, concat_axis=0, tiled=True)

    old_ids = take(request_order)
    sources = old_ids // rows_here
    lengths = request_lengths[old_ids]
    counts = retained_counts[old_ids]
    keep = jnp.where(slot_index[None, :] < counts[:, None], retained_positions[old_ids], CAP)
    spots = jnp.arange(CAP, dtype=jnp.int32)
    dropped = (spots[None, :] < lengths[:, None]) & jnp.logical_not(
        jnp.any(keep[:, :, None] == spots[None, None, :], axis=1)
    )
    dropped_weight = jnp.where(dropped, blended_weight[old_ids], 0.0)
    dropped_mass = jnp.log(1.0 + jnp.sum(dropped_weight.reshape(rows_here, PAGES, PAGE), axis=2))
    page_start = jnp.arange(PAGES, dtype=jnp.int32) * PAGE
    bias_slots = jnp.concatenate(
        [
            jnp.where(slot_index[None, :] < counts[:, None], 0.0, NEG),
            jnp.where(page_start[None, :] < lengths[:, None], dropped_mass, NEG),
        ],
        axis=1,
    )
    columns = jnp.arange(ROWS, dtype=jnp.int32) % LANES
    head_rows = jnp.arange(8, dtype=jnp.int32)
    bias = jnp.where(
        columns[None, None, :] == 2 * head_rows[None, :, None],
        jnp.repeat(bias_slots, LANES, axis=1)[:, None, :],
        NEG,
    )
    bias = jnp.pad(bias, ((0, 0), (0, 0), (0, PAD_ROWS - ROWS)), constant_values=NEG)

    gathered = lax.all_gather(hidden_in, "head", axis=1, tiled=True)
    normed = layer_norm(gathered.astype(jnp.float32)).astype(jnp.bfloat16)
    project = lambda index: jnp.dot(
        normed, qkv_weight[:, index], preferred_element_type=jnp.float32
    ).reshape(rows_here, heads_here, HEAD_DIM)
    pad_heads = lambda array: jnp.pad(
        array.astype(jnp.bfloat16), ((0, 0), (0, 8 - heads_here), (0, 0))
    )
    queries = pad_heads(rotate(project(0), lengths))
    new_keys = pad_heads(rotate(project(1), lengths))
    new_values = pad_heads(project(2))

    packed, share = attend(
        sources, queries, new_keys, new_values, bias, out_weight, arrived, peers
    )
    parts = lax.all_to_all(share, "head", split_axis=0, concat_axis=0, tiled=True)
    summed = jnp.sum(parts.astype(jnp.float32), axis=0)
    hidden_out = (hidden_in.astype(jnp.float32) + summed).astype(jnp.bfloat16)
    packed_cache = (
        packed.reshape(rows_here, SLOTS, heads_here, 2, HEAD_DIM)
        .transpose(0, 1, 3, 2, 4)
        .reshape(rows_here, SLOTS, 2, head_width)
    )
    return (hidden_out, packed_cache)


def solution(mesh):
    return jax.shard_map(
        local,
        mesh=mesh,
        in_specs=(
            P("blk", "head"),
            P(None, None, "head"),
            P("head", None),
            P("blk", None, None, "head"),
            P("blk", None),
            P(),
            P(),
            P(),
            P(),
            P(),
        ),
        out_specs=(P("blk", "head"), P("blk", None, None, "head")),
        check_vma=False,
    )
```

```python
import jax
import jax.numpy as jnp
from jax import lax
from jax.experimental import pallas as pl
from jax.experimental.pallas import tpu as pltpu
from jax.sharding import PartitionSpec as P

HEAD_DIM = 128
PAGE = 64
PAGES = 4
CAP = 256
KEPT = 128
SLOTS = 132
HEADS_HERE = 2
LANES = HEADS_HERE * 2
ROWS = SLOTS * LANES
PAD_ROWS = 640
NEG = -1e30

epsilon = 1e-05


def layer_norm(hidden):
    average = jnp.mean(hidden, axis=-1, keepdims=True)
    centered = hidden - average
    variance = jnp.mean(centered * centered, axis=-1, keepdims=True)
    return centered * lax.rsqrt(variance + epsilon)


def rotate(vectors, positions):
    half_dim = vectors.shape[-1] // 2
    inverse_freq = 10000.0 ** (-jnp.arange(half_dim, dtype=jnp.float32) / half_dim)
    angles = positions.astype(jnp.float32)[:, None, None] * inverse_freq
    cosine = jnp.cos(angles)
    sine_part = jnp.sin(angles)
    first_half = vectors[..., :half_dim]
    second_half = vectors[..., half_dim:]
    return jnp.concatenate(
        [
            first_half * cosine - second_half * sine_part,
            second_half * cosine + first_half * sine_part,
        ],
        axis=-1,
    )


def pack_kernel(
    block_ref,
    page_hbm,
    length_hbm,
    count_hbm,
    order_hbm,
    keep_hbm,
    weight_hbm,
    cache_rows_hbm,
    cache_flat_hbm,
    send_hbm,
    rows_vmem,
    flat_vmem,
    out_vmem,
    wide_vmem,
    order_vmem,
    keep_vmem,
    weight_vmem,
    spot_vmem,
    page_smem,
    length_smem,
    count_smem,
    spot_smem,
    small_sem,
    load_sem,
    spot_sem,
    out_sem,
):
    count = keep_vmem.shape[0]
    pool_rows = cache_rows_hbm.shape[0]
    first = pl.multiple_of(block_ref[0] * count, count)
    small = [
        pltpu.make_async_copy(source, target, small_sem.at[n])
        for n, (source, target) in enumerate(
            [
                (keep_hbm.at[pl.ds(first, count)], keep_vmem),
                (count_hbm, count_smem),
                (page_hbm, page_smem),
                (order_hbm, order_vmem),
                (length_hbm, length_smem),
                (weight_hbm.at[pl.ds(first, count)], weight_vmem),
            ]
        )
    ]
    for copy in small:
        copy.start()
    load_rows = pltpu.make_async_copy(
        cache_rows_hbm, rows_vmem.at[pl.ds(0, pool_rows)], load_sem.at[0]
    )
    load_flat = pltpu.make_async_copy(cache_flat_hbm, flat_vmem, load_sem.at[1])
    load_rows.start()
    load_flat.start()
    for copy in small:
        copy.wait()

    keep = keep_vmem[...]
    slot_id = lax.broadcasted_iota(jnp.int32, keep.shape, 1)
    row_id = lax.broadcasted_iota(jnp.int32, keep.shape, 0)
    counts = jnp.zeros(keep.shape, jnp.int32)
    base = jnp.zeros(keep.shape, jnp.int32)
    page_of = keep >> 6
    for i in range(count):
        here = row_id == i
        counts = jnp.where(here, count_smem[first + i], counts)
        for j in range(PAGES):
            base = jnp.where(here & (page_of == j), page_smem[j, i] * PAGE, base)
    keep = jnp.where(slot_id < counts, keep, CAP)
    spot_vmem[...] = jnp.where(slot_id < counts, base + (keep & (PAGE - 1)), pool_rows)
    move_spots = pltpu.make_async_copy(spot_vmem, spot_smem, spot_sem)
    move_spots.start()

    order = order_vmem[...]
    place = (
        lax.broadcasted_iota(jnp.int32, order.shape, 0) * order.shape[1]
        + lax.broadcasted_iota(jnp.int32, order.shape, 1)
    ) // count
    targets = [jnp.sum(jnp.where(order == first + i, place, 0)) for i in range(count)]

    keep_cols = jnp.transpose(keep.astype(jnp.float32))
    lane_pos = lax.broadcasted_iota(jnp.int32, (KEPT, CAP), 1).astype(jnp.float32)
    spot = lax.broadcasted_iota(jnp.int32, (1, CAP), 1)
    factors = []
    for i in range(count):
        match = keep_cols[:, i : i + 1] == lane_pos
        kept = jnp.max(jnp.where(match, 1.0, 0.0), axis=0, keepdims=True)
        dropped = (spot < length_smem[first + i]) & (kept < 0.5)
        factors.append(jnp.where(dropped, weight_vmem[i : i + 1, :], 0.0))
    factors = jnp.concatenate(factors, axis=0).astype(jnp.bfloat16)
    spread = (
        lax.broadcasted_iota(jnp.int32, (CAP, CAP * LANES), 1) >> 2
        == lax.broadcasted_iota(jnp.int32, (CAP, CAP * LANES), 0)
    )
    spread = jnp.where(spread, 1.0, 0.0).astype(jnp.bfloat16)
    wide_vmem[...] = jnp.dot(factors, spread, preferred_element_type=jnp.float32)
    page_lanes = PAGE * LANES
    out_row = lax.broadcasted_iota(jnp.int32, (PAGES * LANES, page_lanes), 0)
    out_lane = lax.broadcasted_iota(jnp.int32, (PAGES * LANES, page_lanes), 1)
    same = (out_row & (LANES - 1)) == (out_lane & (LANES - 1))
    selectors = [jnp.where(same & (out_row >> 2 == j), 1.0, 0.0) for j in range(PAGES)]

    load_flat.wait()
    for i in range(count):
        merged = jnp.zeros((PAGES * LANES, HEAD_DIM), jnp.float32)
        for j in range(PAGES):
            wide = wide_vmem[i : i + 1, j * page_lanes : (j + 1) * page_lanes]
            merged = merged + jnp.dot(
                (selectors[j] * wide).astype(jnp.bfloat16),
                flat_vmem[page_smem[j, i]],
                preferred_element_type=jnp.float32,
            )
        out_vmem[i, pl.ds(KEPT, PAGES)] = merged.astype(jnp.bfloat16).reshape(
            PAGES, LANES, HEAD_DIM
        )

    zero_row = jnp.zeros((LANES, HEAD_DIM), jnp.bfloat16)
    rows_vmem[pool_rows] = zero_row
    move_spots.wait()
    load_rows.wait()
    group = 16
    copies = [
        pltpu.make_async_copy(out_vmem.at[i], send_hbm.at[targets[i]], out_sem.at[i])
        for i in range(count)
    ]
    for i in range(count):

        def gather(c, carry):
            picked = [rows_vmem[spot_smem[i, c * group + u]] for u in range(group)]
            for u in range(group):
                out_vmem[i, c * group + u] = picked[u]
            return carry

        def clear(c, carry):
            for u in range(group):
                out_vmem[i, c * group + u] = zero_row
            return carry

        full = (count_smem[first + i] + group - 1) >> 4
        lax.fori_loop(0, full, gather, 0)
        lax.fori_loop(full, KEPT // group, clear, 0)
        copies[i].start()
    for copy in copies:
        copy.wait()


def pack(block_index, page_table, lengths, counts, order, positions, weights, cache_pool, blocks):
    count = page_table.shape[0]
    pool = cache_pool.shape[0]
    view = cache_pool.reshape(pool, PAGE, 2, HEADS_HERE, HEAD_DIM).transpose(0, 1, 3, 2, 4)
    as_rows = view.reshape(pool * PAGE, LANES, HEAD_DIM)
    as_flat = view.reshape(pool, PAGE * LANES, HEAD_DIM)
    requests = order.shape[0]
    hbm = lambda: pl.BlockSpec(memory_space=pltpu.HBM)
    operands = [
        page_table.T,
        lengths,
        counts,
        order.reshape(requests // 128, 128),
        positions,
        weights,
        as_rows,
        as_flat,
    ]
    operands = [pltpu.with_memory_space_constraint(x, pltpu.HBM) for x in operands]
    return pl.pallas_call(
        pack_kernel,
        out_shape=pltpu.HBM((blocks, SLOTS, LANES, HEAD_DIM), jnp.bfloat16),
        grid_spec=pltpu.PrefetchScalarGridSpec(
            num_scalar_prefetch=1,
            grid=(),
            in_specs=[hbm() for _ in operands],
            out_specs=hbm(),
            scratch_shapes=[
                pltpu.VMEM((pool * PAGE + 1, LANES, HEAD_DIM), jnp.bfloat16),
                pltpu.VMEM((pool, PAGE * LANES, HEAD_DIM), jnp.bfloat16),
                pltpu.VMEM((count, SLOTS, LANES, HEAD_DIM), jnp.bfloat16),
                pltpu.VMEM((count, CAP * LANES), jnp.float32),
                pltpu.VMEM((requests // 128, 128), jnp.int32),
                pltpu.VMEM((count, KEPT), jnp.int32),
                pltpu.VMEM((count, CAP), jnp.float32),
                pltpu.VMEM((count, KEPT), jnp.int32),
                pltpu.SMEM((PAGES, count), jnp.int32),
                pltpu.SMEM((requests,), jnp.int32),
                pltpu.SMEM((requests,), jnp.int32),
                pltpu.SMEM((count, KEPT), jnp.int32),
                pltpu.SemaphoreType.DMA((6,)),
                pltpu.SemaphoreType.DMA((2,)),
                pltpu.SemaphoreType.DMA(()),
                pltpu.SemaphoreType.DMA((count,)),
            ],
        ),
        compiler_params=pltpu.CompilerParams(vmem_limit_bytes=24 * 1024 * 1024),
        name="pack",
    )(jnp.reshape(block_index, (1,)), *operands)


def attend_kernel(
    source_ref,
    query_ref,
    key_ref,
    value_ref,
    bias_ref,
    weight_ref,
    recv_hbm,
    packed_hbm,
    share_ref,
    rows_vmem,
    score_vmem,
    attended_vmem,
    in_sem,
    out_sem,
):
    count = query_ref.shape[0]
    group = query_ref.shape[1]
    ins = [
        pltpu.make_async_copy(
            recv_hbm.at[source_ref[r]], rows_vmem.at[r, pl.ds(0, ROWS)], in_sem.at[r]
        )
        for r in range(count)
    ]
    outs = [
        pltpu.make_async_copy(rows_vmem.at[r, pl.ds(0, ROWS)], packed_hbm.at[r], out_sem.at[r])
        for r in range(count)
    ]
    for r in range(count):
        ins[r].start()
    for r in range(count):
        rows_vmem[r, pl.ds(ROWS, PAD_ROWS - ROWS)] = jnp.zeros(
            (PAD_ROWS - ROWS, HEAD_DIM), jnp.bfloat16
        )
    scale = HEAD_DIM ** (-0.5)
    contract_last = (((1,), (1,)), ((), ()))
    own_score = (
        jnp.sum(
            query_ref[...].astype(jnp.float32) * key_ref[...].astype(jnp.float32),
            axis=-1,
            keepdims=True,
        )
        * scale
    ).reshape(count * group, 1)
    for r in range(count):
        ins[r].wait()
        outs[r].start()
        scores = lax.dot_general(
            query_ref[r], rows_vmem[r], contract_last, preferred_element_type=jnp.float32
        )
        score_vmem[r * group : (r + 1) * group, :] = scores * scale + bias_ref[r]
    scores = score_vmem[...]
    highest = jnp.maximum(jnp.max(scores, axis=-1, keepdims=True), own_score)
    exponentials = jnp.exp(scores - highest)
    own_exp = jnp.exp(own_score - highest)
    denominator = jnp.sum(exponentials, axis=-1, keepdims=True) + own_exp
    probabilities = exponentials / denominator
    own_prob = (own_exp / denominator).astype(jnp.bfloat16).astype(jnp.float32)
    score_vmem[...] = pltpu.roll(probabilities, 1, axis=1)
    for r in range(count):
        moved = score_vmem[r * group : (r + 1) * group, :].astype(jnp.bfloat16)
        combined = jnp.dot(moved, rows_vmem[r], preferred_element_type=jnp.float32)
        attended_vmem[r] = combined + own_prob[
            r * group : (r + 1) * group
        ] * value_ref[r].astype(jnp.float32)
    attended = jnp.concatenate(
        [attended_vmem[:, h, :] for h in range(HEADS_HERE)], axis=1
    ).astype(jnp.bfloat16)
    share = jnp.dot(attended, weight_ref[...], preferred_element_type=jnp.float32).astype(
        jnp.bfloat16
    )
    width = share_ref.shape[2]
    for e in range(share_ref.shape[0]):
        share_ref[e] = share[:, e * width : (e + 1) * width]
    for r in range(count):
        outs[r].wait()


def attend(sources, queries, keys, values, bias, out_weight, recv, peers):
    count, group = queries.shape[:2]
    width = out_weight.shape[1] // peers
    whole = lambda: pl.BlockSpec(memory_space=pltpu.VMEM)
    hbm = lambda: pl.BlockSpec(memory_space=pltpu.HBM)
    return pl.pallas_call(
        attend_kernel,
        out_shape=(
            pltpu.HBM((count, ROWS, HEAD_DIM), jnp.bfloat16),
            jax.ShapeDtypeStruct((peers, count, width), jnp.bfloat16),
        ),
        grid_spec=pltpu.PrefetchScalarGridSpec(
            num_scalar_prefetch=1,
            grid=(),
            in_specs=[whole(), whole(), whole(), whole(), whole(), hbm()],
            out_specs=[hbm(), whole()],
            scratch_shapes=[
                pltpu.VMEM((count, PAD_ROWS, HEAD_DIM), jnp.bfloat16),
                pltpu.VMEM((count * group, PAD_ROWS), jnp.float32),
                pltpu.VMEM((count, group, HEAD_DIM), jnp.float32),
                pltpu.SemaphoreType.DMA((count,)),
                pltpu.SemaphoreType.DMA((count,)),
            ],
        ),
        compiler_params=pltpu.CompilerParams(vmem_limit_bytes=16 * 1024 * 1024),
        name="attend",
    )(sources, queries, keys, values, bias, out_weight, recv)


def local(
    hidden_in,
    qkv_weight,
    out_weight,
    cache_pool,
    page_table,
    request_order,
    request_lengths,
    retained_counts,
    retained_positions,
    blended_weight,
):
    rows_here = hidden_in.shape[0]
    head_width = qkv_weight.shape[2]
    heads_here = head_width // HEAD_DIM
    blocks = lax.axis_size("blk")
    peers = lax.axis_size("head")
    block_index = lax.axis_index("blk")
    first = block_index * rows_here
    slot_index = jnp.arange(KEPT, dtype=jnp.int32)
    take = lambda array: lax.dynamic_slice_in_dim(array, first, rows_here, 0)

    outgoing = pack(
        block_index,
        page_table,
        request_lengths,
        retained_counts,
        request_order,
        retained_positions,
        blended_weight,
        cache_pool,
        blocks,
    )
    outgoing = outgoing.reshape(blocks, ROWS, HEAD_DIM)
    arrived = lax.all_to_all(outgoing, "blk", split_axis=0, concat_axis=0, tiled=True)

    old_ids = take(request_order)
    sources = old_ids // rows_here
    lengths = request_lengths[old_ids]
    counts = retained_counts[old_ids]
    keep = jnp.where(slot_index[None, :] < counts[:, None], retained_positions[old_ids], CAP)
    spots = jnp.arange(CAP, dtype=jnp.int32)
    dropped = (spots[None, :] < lengths[:, None]) & jnp.logical_not(
        jnp.any(keep[:, :, None] == spots[None, None, :], axis=1)
    )
    dropped_weight = jnp.where(dropped, blended_weight[old_ids], 0.0)
    dropped_mass = jnp.log(1.0 + jnp.sum(dropped_weight.reshape(rows_here, PAGES, PAGE), axis=2))
    page_start = jnp.arange(PAGES, dtype=jnp.int32) * PAGE
    bias_slots = jnp.concatenate(
        [
            jnp.where(slot_index[None, :] < counts[:, None], 0.0, NEG),
            jnp.where(page_start[None, :] < lengths[:, None], dropped_mass, NEG),
        ],
        axis=1,
    )
    columns = jnp.arange(ROWS, dtype=jnp.int32) % LANES
    head_rows = jnp.arange(8, dtype=jnp.int32)
    bias = jnp.where(
        columns[None, None, :] == 2 * head_rows[None, :, None],
        jnp.repeat(bias_slots, LANES, axis=1)[:, None, :],
        NEG,
    )
    bias = jnp.pad(bias, ((0, 0), (0, 0), (0, PAD_ROWS - ROWS)), constant_values=NEG)

    gathered = lax.all_gather(hidden_in, "head", axis=1, tiled=True)
    normed = layer_norm(gathered.astype(jnp.float32)).astype(jnp.bfloat16)
    project = lambda index: jnp.dot(
        normed, qkv_weight[:, index], preferred_element_type=jnp.float32
    ).reshape(rows_here, heads_here, HEAD_DIM)
    pad_heads = lambda array: jnp.pad(
        array.astype(jnp.bfloat16), ((0, 0), (0, 8 - heads_here), (0, 0))
    )
    queries = pad_heads(rotate(project(0), lengths))
    new_keys = pad_heads(rotate(project(1), lengths))
    new_values = pad_heads(project(2))

    packed, share = attend(
        sources, queries, new_keys, new_values, bias, out_weight, arrived, peers
    )
    parts = lax.all_to_all(share, "head", split_axis=0, concat_axis=0, tiled=True)
    summed = jnp.sum(parts.astype(jnp.float32), axis=0)
    hidden_out = (hidden_in.astype(jnp.float32) + summed).astype(jnp.bfloat16)
    packed_cache = (
        packed.reshape(rows_here, SLOTS, heads_here, 2, HEAD_DIM)
        .transpose(0, 1, 3, 2, 4)
        .reshape(rows_here, SLOTS, 2, head_width)
    )
    return (hidden_out, packed_cache)


def solution(mesh):
    return jax.shard_map(
        local,
        mesh=mesh,
        in_specs=(
            P("blk", "head"),
            P(None, None, "head"),
            P("head", None),
            P("blk", None, None, "head"),
            P("blk", None),
            P(),
            P(),
            P(),
            P(),
            P(),
        ),
        out_specs=(P("blk", "head"), P("blk", None, None, "head")),
        check_vma=False,
    )
```

```python
import jax
import jax.numpy as jnp
from jax import lax
from jax.experimental import pallas as pl
from jax.experimental.pallas import tpu as pltpu
from jax.sharding import PartitionSpec as P

HEAD_DIM = 128
PAGE = 64
PAGES = 4
CAP = 256
KEPT = 128
SLOTS = 132
HEADS_HERE = 2
LANES = HEADS_HERE * 2
ROWS = SLOTS * LANES
PAD_ROWS = 640
NEG = -1e30

epsilon = 1e-05


def layer_norm(hidden):
    average = jnp.mean(hidden, axis=-1, keepdims=True)
    centered = hidden - average
    variance = jnp.mean(centered * centered, axis=-1, keepdims=True)
    return centered * lax.rsqrt(variance + epsilon)


def rotate(vectors, positions):
    half_dim = vectors.shape[-1] // 2
    inverse_freq = 10000.0 ** (-jnp.arange(half_dim, dtype=jnp.float32) / half_dim)
    angles = positions.astype(jnp.float32)[:, None, None] * inverse_freq
    cosine = jnp.cos(angles)
    sine_part = jnp.sin(angles)
    first_half = vectors[..., :half_dim]
    second_half = vectors[..., half_dim:]
    return jnp.concatenate(
        [
            first_half * cosine - second_half * sine_part,
            second_half * cosine + first_half * sine_part,
        ],
        axis=-1,
    )


def pack_kernel(
    block_ref,
    page_hbm,
    length_hbm,
    count_hbm,
    order_hbm,
    keep_hbm,
    weight_hbm,
    cache_rows_hbm,
    cache_flat_hbm,
    send_hbm,
    rows_vmem,
    flat_vmem,
    out_vmem,
    wide_vmem,
    order_vmem,
    keep_vmem,
    weight_vmem,
    spot_vmem,
    page_smem,
    length_smem,
    count_smem,
    spot_smem,
    small_sem,
    load_sem,
    spot_sem,
    out_sem,
):
    count = keep_vmem.shape[0]
    group = 16
    pool_rows = cache_rows_hbm.shape[0]
    first = pl.multiple_of(block_ref[0] * count, count)
    small = [
        pltpu.make_async_copy(source, target, small_sem.at[n])
        for n, (source, target) in enumerate(
            [
                (keep_hbm.at[pl.ds(first, count)], keep_vmem),
                (count_hbm, count_smem),
                (page_hbm, page_smem),
                (order_hbm, order_vmem),
                (length_hbm, length_smem),
                (weight_hbm.at[pl.ds(first, count)], weight_vmem),
            ]
        )
    ]
    for copy in small:
        copy.start()
    load_rows = pltpu.make_async_copy(
        cache_rows_hbm, rows_vmem.at[pl.ds(0, pool_rows)], load_sem.at[0]
    )
    load_flat = pltpu.make_async_copy(cache_flat_hbm, flat_vmem, load_sem.at[1])
    load_rows.start()
    for copy in small:
        copy.wait()
    load_flat.start()

    keep = keep_vmem[...]
    slot_id = lax.broadcasted_iota(jnp.int32, keep.shape, 1)
    row_id = lax.broadcasted_iota(jnp.int32, keep.shape, 0)
    counts = jnp.zeros(keep.shape, jnp.int32)
    base = jnp.zeros(keep.shape, jnp.int32)
    page_of = keep >> 6
    for i in range(count):
        here = row_id == i
        counts = jnp.where(here, count_smem[first + i], counts)
        for j in range(PAGES):
            base = jnp.where(here & (page_of == j), page_smem[j, i] * PAGE, base)
    keep = jnp.where(slot_id < counts, keep, CAP)
    spot_vmem[...] = jnp.where(slot_id < counts, base + (keep & (PAGE - 1)), pool_rows)
    move_spots = pltpu.make_async_copy(spot_vmem, spot_smem, spot_sem)
    move_spots.start()

    order = order_vmem[...]
    place = (
        lax.broadcasted_iota(jnp.int32, order.shape, 0) * order.shape[1]
        + lax.broadcasted_iota(jnp.int32, order.shape, 1)
    ) // count
    targets = [jnp.sum(jnp.where(order == first + i, place, 0)) for i in range(count)]

    keep_cols = jnp.transpose(keep.astype(jnp.float32))
    lane_pos = lax.broadcasted_iota(jnp.int32, (KEPT, CAP), 1).astype(jnp.float32)
    spot = lax.broadcasted_iota(jnp.int32, (1, CAP), 1)
    factors = []
    for i in range(count):
        match = keep_cols[:, i : i + 1] == lane_pos
        kept = jnp.max(jnp.where(match, 1.0, 0.0), axis=0, keepdims=True)
        dropped = (spot < length_smem[first + i]) & (kept < 0.5)
        factors.append(jnp.where(dropped, weight_vmem[i : i + 1, :], 0.0))
    factors = jnp.concatenate(factors, axis=0).astype(jnp.bfloat16)
    spread = (
        lax.broadcasted_iota(jnp.int32, (CAP, CAP * LANES), 1) >> 2
        == lax.broadcasted_iota(jnp.int32, (CAP, CAP * LANES), 0)
    )
    spread = jnp.where(spread, 1.0, 0.0).astype(jnp.bfloat16)
    wide_vmem[...] = jnp.dot(factors, spread, preferred_element_type=jnp.float32)
    page_lanes = PAGE * LANES
    out_row = lax.broadcasted_iota(jnp.int32, (PAGES * LANES, page_lanes), 0)
    out_lane = lax.broadcasted_iota(jnp.int32, (PAGES * LANES, page_lanes), 1)
    same = (out_row & (LANES - 1)) == (out_lane & (LANES - 1))
    selectors = [jnp.where(same & (out_row >> 2 == j), 1.0, 0.0) for j in range(PAGES)]

    zero_rows = jnp.zeros((group, LANES, HEAD_DIM), jnp.bfloat16)
    rows_vmem[pool_rows] = zero_rows[0]

    def clear(c, carry):
        for i in range(count):
            out_vmem[i, pl.ds(pl.multiple_of(c * group, group), group)] = zero_rows
        return carry

    lax.fori_loop(0, KEPT // group, clear, 0)
    move_spots.wait()
    load_rows.wait()
    for i in range(count):

        def gather(c, carry):
            picked = [rows_vmem[spot_smem[i, c * group + u]] for u in range(group)]
            for u in range(group):
                out_vmem[i, c * group + u] = picked[u]
            return carry

        full = (count_smem[first + i] + group - 1) >> 4
        lax.fori_loop(0, full, gather, 0)

    copies = [
        pltpu.make_async_copy(out_vmem.at[i], send_hbm.at[targets[i]], out_sem.at[i])
        for i in range(count)
    ]
    load_flat.wait()
    for i in range(count):
        merged = jnp.zeros((PAGES * LANES, HEAD_DIM), jnp.float32)
        for j in range(PAGES):
            wide = wide_vmem[i : i + 1, j * page_lanes : (j + 1) * page_lanes]
            merged = merged + jnp.dot(
                (selectors[j] * wide).astype(jnp.bfloat16),
                flat_vmem[page_smem[j, i]],
                preferred_element_type=jnp.float32,
            )
        out_vmem[i, pl.ds(KEPT, PAGES)] = merged.astype(jnp.bfloat16).reshape(
            PAGES, LANES, HEAD_DIM
        )
        copies[i].start()
    for copy in copies:
        copy.wait()


def pack(block_index, page_table, lengths, counts, order, positions, weights, cache_pool, blocks):
    count = page_table.shape[0]
    pool = cache_pool.shape[0]
    view = cache_pool.reshape(pool, PAGE, 2, HEADS_HERE, HEAD_DIM).transpose(0, 1, 3, 2, 4)
    as_rows = view.reshape(pool * PAGE, LANES, HEAD_DIM)
    as_flat = view.reshape(pool, PAGE * LANES, HEAD_DIM)
    requests = order.shape[0]
    hbm = lambda: pl.BlockSpec(memory_space=pltpu.HBM)
    operands = [
        page_table.T,
        lengths,
        counts,
        order.reshape(requests // 128, 128),
        positions,
        weights,
        as_rows,
        as_flat,
    ]
    operands = [pltpu.with_memory_space_constraint(x, pltpu.HBM) for x in operands]
    return pl.pallas_call(
        pack_kernel,
        out_shape=pltpu.HBM((blocks, SLOTS, LANES, HEAD_DIM), jnp.bfloat16),
        grid_spec=pltpu.PrefetchScalarGridSpec(
            num_scalar_prefetch=1,
            grid=(),
            in_specs=[hbm() for _ in operands],
            out_specs=hbm(),
            scratch_shapes=[
                pltpu.VMEM((pool * PAGE + 1, LANES, HEAD_DIM), jnp.bfloat16),
                pltpu.VMEM((pool, PAGE * LANES, HEAD_DIM), jnp.bfloat16),
                pltpu.VMEM((count, SLOTS, LANES, HEAD_DIM), jnp.bfloat16),
                pltpu.VMEM((count, CAP * LANES), jnp.float32),
                pltpu.VMEM((requests // 128, 128), jnp.int32),
                pltpu.VMEM((count, KEPT), jnp.int32),
                pltpu.VMEM((count, CAP), jnp.float32),
                pltpu.VMEM((count, KEPT), jnp.int32),
                pltpu.SMEM((PAGES, count), jnp.int32),
                pltpu.SMEM((requests,), jnp.int32),
                pltpu.SMEM((requests,), jnp.int32),
                pltpu.SMEM((count, KEPT), jnp.int32),
                pltpu.SemaphoreType.DMA((6,)),
                pltpu.SemaphoreType.DMA((2,)),
                pltpu.SemaphoreType.DMA(()),
                pltpu.SemaphoreType.DMA((count,)),
            ],
        ),
        compiler_params=pltpu.CompilerParams(vmem_limit_bytes=24 * 1024 * 1024),
        name="pack",
    )(jnp.reshape(block_index, (1,)), *operands)


def attend_kernel(
    source_ref,
    query_ref,
    key_ref,
    value_ref,
    bias_ref,
    weight_ref,
    recv_hbm,
    packed_hbm,
    share_ref,
    rows_vmem,
    score_vmem,
    attended_vmem,
    in_sem,
    out_sem,
):
    count = query_ref.shape[0]
    group = query_ref.shape[1]
    ins = [
        pltpu.make_async_copy(
            recv_hbm.at[source_ref[r]], rows_vmem.at[r, pl.ds(0, ROWS)], in_sem.at[r]
        )
        for r in range(count)
    ]
    outs = [
        pltpu.make_async_copy(rows_vmem.at[r, pl.ds(0, ROWS)], packed_hbm.at[r], out_sem.at[r])
        for r in range(count)
    ]
    for r in range(count):
        ins[r].start()
    for r in range(count):
        rows_vmem[r, pl.ds(ROWS, PAD_ROWS - ROWS)] = jnp.zeros(
            (PAD_ROWS - ROWS, HEAD_DIM), jnp.bfloat16
        )
    scale = HEAD_DIM ** (-0.5)
    contract_last = (((1,), (1,)), ((), ()))
    own_score = (
        jnp.sum(
            query_ref[...].astype(jnp.float32) * key_ref[...].astype(jnp.float32),
            axis=-1,
            keepdims=True,
        )
        * scale
    ).reshape(count * group, 1)
    for r in range(count):
        ins[r].wait()
        outs[r].start()
        scores = lax.dot_general(
            query_ref[r], rows_vmem[r], contract_last, preferred_element_type=jnp.float32
        )
        score_vmem[r * group : (r + 1) * group, :] = scores * scale + bias_ref[r]
    scores = score_vmem[...]
    highest = jnp.maximum(jnp.max(scores, axis=-1, keepdims=True), own_score)
    exponentials = jnp.exp(scores - highest)
    own_exp = jnp.exp(own_score - highest)
    denominator = jnp.sum(exponentials, axis=-1, keepdims=True) + own_exp
    probabilities = exponentials / denominator
    own_prob = (own_exp / denominator).astype(jnp.bfloat16).astype(jnp.float32)
    score_vmem[...] = pltpu.roll(probabilities, 1, axis=1)
    for r in range(count):
        moved = score_vmem[r * group : (r + 1) * group, :].astype(jnp.bfloat16)
        combined = jnp.dot(moved, rows_vmem[r], preferred_element_type=jnp.float32)
        attended_vmem[r] = combined + own_prob[
            r * group : (r + 1) * group
        ] * value_ref[r].astype(jnp.float32)
    attended = jnp.concatenate(
        [attended_vmem[:, h, :] for h in range(HEADS_HERE)], axis=1
    ).astype(jnp.bfloat16)
    share = jnp.dot(attended, weight_ref[...], preferred_element_type=jnp.float32).astype(
        jnp.bfloat16
    )
    width = share_ref.shape[2]
    for e in range(share_ref.shape[0]):
        share_ref[e] = share[:, e * width : (e + 1) * width]
    for r in range(count):
        outs[r].wait()


def attend(sources, queries, keys, values, bias, out_weight, recv, peers):
    count, group = queries.shape[:2]
    width = out_weight.shape[1] // peers
    whole = lambda: pl.BlockSpec(memory_space=pltpu.VMEM)
    hbm = lambda: pl.BlockSpec(memory_space=pltpu.HBM)
    return pl.pallas_call(
        attend_kernel,
        out_shape=(
            pltpu.HBM((count, ROWS, HEAD_DIM), jnp.bfloat16),
            jax.ShapeDtypeStruct((peers, count, width), jnp.bfloat16),
        ),
        grid_spec=pltpu.PrefetchScalarGridSpec(
            num_scalar_prefetch=1,
            grid=(),
            in_specs=[whole(), whole(), whole(), whole(), whole(), hbm()],
            out_specs=[hbm(), whole()],
            scratch_shapes=[
                pltpu.VMEM((count, PAD_ROWS, HEAD_DIM), jnp.bfloat16),
                pltpu.VMEM((count * group, PAD_ROWS), jnp.float32),
                pltpu.VMEM((count, group, HEAD_DIM), jnp.float32),
                pltpu.SemaphoreType.DMA((count,)),
                pltpu.SemaphoreType.DMA((count,)),
            ],
        ),
        compiler_params=pltpu.CompilerParams(vmem_limit_bytes=16 * 1024 * 1024),
        name="attend",
    )(sources, queries, keys, values, bias, out_weight, recv)


def local(
    hidden_in,
    qkv_weight,
    out_weight,
    cache_pool,
    page_table,
    request_order,
    request_lengths,
    retained_counts,
    retained_positions,
    blended_weight,
):
    rows_here = hidden_in.shape[0]
    head_width = qkv_weight.shape[2]
    heads_here = head_width // HEAD_DIM
    blocks = lax.axis_size("blk")
    peers = lax.axis_size("head")
    block_index = lax.axis_index("blk")
    first = block_index * rows_here
    slot_index = jnp.arange(KEPT, dtype=jnp.int32)
    take = lambda array: lax.dynamic_slice_in_dim(array, first, rows_here, 0)

    outgoing = pack(
        block_index,
        page_table,
        request_lengths,
        retained_counts,
        request_order,
        retained_positions,
        blended_weight,
        cache_pool,
        blocks,
    )
    outgoing = outgoing.reshape(blocks, ROWS, HEAD_DIM)
    arrived = lax.all_to_all(outgoing, "blk", split_axis=0, concat_axis=0, tiled=True)

    old_ids = take(request_order)
    sources = old_ids // rows_here
    lengths = request_lengths[old_ids]
    counts = retained_counts[old_ids]
    keep = jnp.where(slot_index[None, :] < counts[:, None], retained_positions[old_ids], CAP)
    spots = jnp.arange(CAP, dtype=jnp.int32)
    dropped = (spots[None, :] < lengths[:, None]) & jnp.logical_not(
        jnp.any(keep[:, :, None] == spots[None, None, :], axis=1)
    )
    dropped_weight = jnp.where(dropped, blended_weight[old_ids], 0.0)
    dropped_mass = jnp.log(1.0 + jnp.sum(dropped_weight.reshape(rows_here, PAGES, PAGE), axis=2))
    page_start = jnp.arange(PAGES, dtype=jnp.int32) * PAGE
    bias_slots = jnp.concatenate(
        [
            jnp.where(slot_index[None, :] < counts[:, None], 0.0, NEG),
            jnp.where(page_start[None, :] < lengths[:, None], dropped_mass, NEG),
        ],
        axis=1,
    )
    columns = jnp.arange(ROWS, dtype=jnp.int32) % LANES
    head_rows = jnp.arange(8, dtype=jnp.int32)
    bias = jnp.where(
        columns[None, None, :] == 2 * head_rows[None, :, None],
        jnp.repeat(bias_slots, LANES, axis=1)[:, None, :],
        NEG,
    )
    bias = jnp.pad(bias, ((0, 0), (0, 0), (0, PAD_ROWS - ROWS)), constant_values=NEG)

    gathered = lax.all_gather(hidden_in, "head", axis=1, tiled=True)
    normed = layer_norm(gathered.astype(jnp.float32)).astype(jnp.bfloat16)
    project = lambda index: jnp.dot(
        normed, qkv_weight[:, index], preferred_element_type=jnp.float32
    ).reshape(rows_here, heads_here, HEAD_DIM)
    pad_heads = lambda array: jnp.pad(
        array.astype(jnp.bfloat16), ((0, 0), (0, 8 - heads_here), (0, 0))
    )
    queries = pad_heads(rotate(project(0), lengths))
    new_keys = pad_heads(rotate(project(1), lengths))
    new_values = pad_heads(project(2))

    packed, share = attend(
        sources, queries, new_keys, new_values, bias, out_weight, arrived, peers
    )
    parts = lax.all_to_all(share, "head", split_axis=0, concat_axis=0, tiled=True)
    summed = jnp.sum(parts.astype(jnp.float32), axis=0)
    hidden_out = (hidden_in.astype(jnp.float32) + summed).astype(jnp.bfloat16)
    packed_cache = (
        packed.reshape(rows_here, SLOTS, heads_here, 2, HEAD_DIM)
        .transpose(0, 1, 3, 2, 4)
        .reshape(rows_here, SLOTS, 2, head_width)
    )
    return (hidden_out, packed_cache)


def solution(mesh):
    return jax.shard_map(
        local,
        mesh=mesh,
        in_specs=(
            P("blk", "head"),
            P(None, None, "head"),
            P("head", None),
            P("blk", None, None, "head"),
            P("blk", None),
            P(),
            P(),
            P(),
            P(),
            P(),
        ),
        out_specs=(P("blk", "head"), P("blk", None, None, "head")),
        check_vma=False,
    )
```

```python
import jax
import jax.numpy as jnp
from jax import lax
from jax.experimental import pallas as pl
from jax.experimental.pallas import tpu as pltpu
from jax.sharding import PartitionSpec as P

HEAD_DIM = 128
PAGE = 64
PAGES = 4
CAP = 256
KEPT = 128
SLOTS = 132
HEADS_HERE = 2
LANES = HEADS_HERE * 2
ROWS = SLOTS * LANES
PAD_ROWS = 640
NEG = -1e30
ROUND_ONE = 54
ROUND_TWO = 36
STEP = 6

epsilon = 1e-05


def layer_norm(hidden):
    average = jnp.mean(hidden, axis=-1, keepdims=True)
    centered = hidden - average
    variance = jnp.mean(centered * centered, axis=-1, keepdims=True)
    return centered * lax.rsqrt(variance + epsilon)


def rotate(vectors, positions):
    half_dim = vectors.shape[-1] // 2
    inverse_freq = 10000.0 ** (-jnp.arange(half_dim, dtype=jnp.float32) / half_dim)
    angles = positions.astype(jnp.float32)[:, None, None] * inverse_freq
    cosine = jnp.cos(angles)
    sine_part = jnp.sin(angles)
    first_half = vectors[..., :half_dim]
    second_half = vectors[..., half_dim:]
    return jnp.concatenate(
        [
            first_half * cosine - second_half * sine_part,
            second_half * cosine + first_half * sine_part,
        ],
        axis=-1,
    )


def pack_kernel(
    block_ref,
    page_hbm,
    length_hbm,
    count_hbm,
    order_hbm,
    keep_hbm,
    weight_hbm,
    cache_rows_hbm,
    cache_flat_hbm,
    send_hbm,
    rows_vmem,
    flat_vmem,
    out_vmem,
    wide_vmem,
    order_vmem,
    keep_vmem,
    weight_vmem,
    spot_vmem,
    page_smem,
    length_smem,
    count_smem,
    spot_smem,
    small_sem,
    load_sem,
    spot_sem,
    out_sem,
):
    count = keep_vmem.shape[0]
    group = 16
    pool_rows = cache_rows_hbm.shape[0]
    first = pl.multiple_of(block_ref[0] * count, count)
    small = [
        pltpu.make_async_copy(source, target, small_sem.at[n])
        for n, (source, target) in enumerate(
            [
                (keep_hbm.at[pl.ds(first, count)], keep_vmem),
                (count_hbm, count_smem),
                (page_hbm, page_smem),
                (order_hbm, order_vmem),
                (length_hbm, length_smem),
                (weight_hbm.at[pl.ds(first, count)], weight_vmem),
            ]
        )
    ]
    for copy in small:
        copy.start()
    load_rows = pltpu.make_async_copy(
        cache_rows_hbm, rows_vmem.at[pl.ds(0, pool_rows)], load_sem.at[0]
    )
    load_flat = pltpu.make_async_copy(cache_flat_hbm, flat_vmem, load_sem.at[1])
    load_rows.start()
    for copy in small:
        copy.wait()
    load_flat.start()

    keep = keep_vmem[...]
    slot_id = lax.broadcasted_iota(jnp.int32, keep.shape, 1)
    row_id = lax.broadcasted_iota(jnp.int32, keep.shape, 0)
    counts = jnp.zeros(keep.shape, jnp.int32)
    base = jnp.zeros(keep.shape, jnp.int32)
    page_of = keep >> 6
    for i in range(count):
        here = row_id == i
        counts = jnp.where(here, count_smem[first + i], counts)
        for j in range(PAGES):
            base = jnp.where(here & (page_of == j), page_smem[j, i] * PAGE, base)
    keep = jnp.where(slot_id < counts, keep, CAP)
    spot_vmem[...] = jnp.where(slot_id < counts, base + (keep & (PAGE - 1)), pool_rows)
    move_spots = pltpu.make_async_copy(spot_vmem, spot_smem, spot_sem)
    move_spots.start()

    order = order_vmem[...]
    place = (
        lax.broadcasted_iota(jnp.int32, order.shape, 0) * order.shape[1]
        + lax.broadcasted_iota(jnp.int32, order.shape, 1)
    ) // count
    targets = [jnp.sum(jnp.where(order == first + i, place, 0)) for i in range(count)]

    keep_cols = jnp.transpose(keep.astype(jnp.float32))
    lane_pos = lax.broadcasted_iota(jnp.int32, (KEPT, CAP), 1).astype(jnp.float32)
    spot = lax.broadcasted_iota(jnp.int32, (1, CAP), 1)
    factors = []
    for i in range(count):
        match = keep_cols[:, i : i + 1] == lane_pos
        kept = jnp.max(jnp.where(match, 1.0, 0.0), axis=0, keepdims=True)
        dropped = (spot < length_smem[first + i]) & (kept < 0.5)
        factors.append(jnp.where(dropped, weight_vmem[i : i + 1, :], 0.0))
    factors = jnp.concatenate(factors, axis=0).astype(jnp.bfloat16)
    spread = (
        lax.broadcasted_iota(jnp.int32, (CAP, CAP * LANES), 1) >> 2
        == lax.broadcasted_iota(jnp.int32, (CAP, CAP * LANES), 0)
    )
    spread = jnp.where(spread, 1.0, 0.0).astype(jnp.bfloat16)
    wide_vmem[...] = jnp.dot(factors, spread, preferred_element_type=jnp.float32)
    page_lanes = PAGE * LANES
    out_row = lax.broadcasted_iota(jnp.int32, (PAGES * LANES, page_lanes), 0)
    out_lane = lax.broadcasted_iota(jnp.int32, (PAGES * LANES, page_lanes), 1)
    same = (out_row & (LANES - 1)) == (out_lane & (LANES - 1))
    selectors = [jnp.where(same & (out_row >> 2 == j), 1.0, 0.0) for j in range(PAGES)]

    zero_rows = jnp.zeros((group, LANES, HEAD_DIM), jnp.bfloat16)
    rows_vmem[pool_rows] = zero_rows[0]

    def clear(c, carry):
        for i in range(count):
            out_vmem[i, pl.ds(pl.multiple_of(c * group, group), group)] = zero_rows
        return carry

    lax.fori_loop(0, KEPT // group, clear, 0)
    move_spots.wait()
    load_rows.wait()
    for i in range(count):

        def gather(c, carry):
            picked = [rows_vmem[spot_smem[i, c * group + u]] for u in range(group)]
            for u in range(group):
                out_vmem[i, c * group + u] = picked[u]
            return carry

        full = (count_smem[first + i] + group - 1) >> 4
        lax.fori_loop(0, full, gather, 0)

    copies = [
        pltpu.make_async_copy(out_vmem.at[i], send_hbm.at[targets[i]], out_sem.at[i])
        for i in range(count)
    ]
    load_flat.wait()
    for i in range(count):
        merged = jnp.zeros((PAGES * LANES, HEAD_DIM), jnp.float32)
        for j in range(PAGES):
            wide = wide_vmem[i : i + 1, j * page_lanes : (j + 1) * page_lanes]
            merged = merged + jnp.dot(
                (selectors[j] * wide).astype(jnp.bfloat16),
                flat_vmem[page_smem[j, i]],
                preferred_element_type=jnp.float32,
            )
        out_vmem[i, pl.ds(KEPT, PAGES)] = merged.astype(jnp.bfloat16).reshape(
            PAGES, LANES, HEAD_DIM
        )
        copies[i].start()
    for copy in copies:
        copy.wait()


def pack(block_index, page_table, lengths, counts, order, positions, weights, cache_pool, blocks):
    count = page_table.shape[0]
    pool = cache_pool.shape[0]
    view = cache_pool.reshape(pool, PAGE, 2, HEADS_HERE, HEAD_DIM).transpose(0, 1, 3, 2, 4)
    as_rows = view.reshape(pool * PAGE, LANES, HEAD_DIM)
    as_flat = view.reshape(pool, PAGE * LANES, HEAD_DIM)
    requests = order.shape[0]
    hbm = lambda: pl.BlockSpec(memory_space=pltpu.HBM)
    operands = [
        page_table.T,
        lengths,
        counts,
        order.reshape(requests // 128, 128),
        positions,
        weights,
        as_rows,
        as_flat,
    ]
    operands = [pltpu.with_memory_space_constraint(x, pltpu.HBM) for x in operands]
    return pl.pallas_call(
        pack_kernel,
        out_shape=pltpu.HBM((blocks, SLOTS, LANES, HEAD_DIM), jnp.bfloat16),
        grid_spec=pltpu.PrefetchScalarGridSpec(
            num_scalar_prefetch=1,
            grid=(),
            in_specs=[hbm() for _ in operands],
            out_specs=hbm(),
            scratch_shapes=[
                pltpu.VMEM((pool * PAGE + 1, LANES, HEAD_DIM), jnp.bfloat16),
                pltpu.VMEM((pool, PAGE * LANES, HEAD_DIM), jnp.bfloat16),
                pltpu.VMEM((count, SLOTS, LANES, HEAD_DIM), jnp.bfloat16),
                pltpu.VMEM((count, CAP * LANES), jnp.float32),
                pltpu.VMEM((requests // 128, 128), jnp.int32),
                pltpu.VMEM((count, KEPT), jnp.int32),
                pltpu.VMEM((count, CAP), jnp.float32),
                pltpu.VMEM((count, KEPT), jnp.int32),
                pltpu.SMEM((PAGES, count), jnp.int32),
                pltpu.SMEM((requests,), jnp.int32),
                pltpu.SMEM((requests,), jnp.int32),
                pltpu.SMEM((count, KEPT), jnp.int32),
                pltpu.SemaphoreType.DMA((6,)),
                pltpu.SemaphoreType.DMA((2,)),
                pltpu.SemaphoreType.DMA(()),
                pltpu.SemaphoreType.DMA((count,)),
            ],
        ),
        compiler_params=pltpu.CompilerParams(vmem_limit_bytes=24 * 1024 * 1024),
        name="pack",
    )(jnp.reshape(block_index, (1,)), *operands)


def attend_kernel(
    source_ref,
    query_ref,
    key_ref,
    value_ref,
    bias_ref,
    weight_ref,
    recv_hbm,
    packed_hbm,
    share_ref,
    rows_vmem,
    score_vmem,
    attended_vmem,
    in_sem,
    out_sem,
):
    count = query_ref.shape[0]
    group = query_ref.shape[1]
    ins = [
        pltpu.make_async_copy(
            recv_hbm.at[source_ref[r]], rows_vmem.at[r, pl.ds(0, ROWS)], in_sem.at[r]
        )
        for r in range(count)
    ]
    outs = [
        pltpu.make_async_copy(rows_vmem.at[r, pl.ds(0, ROWS)], packed_hbm.at[r], out_sem.at[r])
        for r in range(count)
    ]
    for r in range(count):
        ins[r].start()
    for r in range(count):
        rows_vmem[r, pl.ds(ROWS, PAD_ROWS - ROWS)] = jnp.zeros(
            (PAD_ROWS - ROWS, HEAD_DIM), jnp.bfloat16
        )
    scale = HEAD_DIM ** (-0.5)
    contract_last = (((1,), (1,)), ((), ()))
    own_score = (
        jnp.sum(
            query_ref[...].astype(jnp.float32) * key_ref[...].astype(jnp.float32),
            axis=-1,
            keepdims=True,
        )
        * scale
    ).reshape(count * group, 1)
    for r in range(count):
        ins[r].wait()
        outs[r].start()
        scores = lax.dot_general(
            query_ref[r], rows_vmem[r], contract_last, preferred_element_type=jnp.float32
        )
        score_vmem[r * group : (r + 1) * group, :] = scores * scale + bias_ref[r]
    scores = score_vmem[...]
    highest = jnp.maximum(jnp.max(scores, axis=-1, keepdims=True), own_score)
    exponentials = jnp.exp(scores - highest)
    own_exp = jnp.exp(own_score - highest)
    denominator = jnp.sum(exponentials, axis=-1, keepdims=True) + own_exp
    probabilities = exponentials / denominator
    own_prob = (own_exp / denominator).astype(jnp.bfloat16).astype(jnp.float32)
    score_vmem[...] = pltpu.roll(probabilities, 1, axis=1)
    for r in range(count):
        moved = score_vmem[r * group : (r + 1) * group, :].astype(jnp.bfloat16)
        combined = jnp.dot(moved, rows_vmem[r], preferred_element_type=jnp.float32)
        attended_vmem[r] = combined + own_prob[
            r * group : (r + 1) * group
        ] * value_ref[r].astype(jnp.float32)
    attended = jnp.concatenate(
        [attended_vmem[:, h, :] for h in range(HEADS_HERE)], axis=1
    ).astype(jnp.bfloat16)
    share = jnp.dot(attended, weight_ref[...], preferred_element_type=jnp.float32).astype(
        jnp.bfloat16
    )
    width = share_ref.shape[2]
    for e in range(share_ref.shape[0]):
        share_ref[e] = share[:, e * width : (e + 1) * width]
    for r in range(count):
        outs[r].wait()


def attend(sources, queries, keys, values, bias, out_weight, recv, peers):
    count, group = queries.shape[:2]
    width = out_weight.shape[1] // peers
    whole = lambda: pl.BlockSpec(memory_space=pltpu.VMEM)
    hbm = lambda: pl.BlockSpec(memory_space=pltpu.HBM)
    return pl.pallas_call(
        attend_kernel,
        out_shape=(
            pltpu.HBM((count, ROWS, HEAD_DIM), jnp.bfloat16),
            jax.ShapeDtypeStruct((peers, count, width), jnp.bfloat16),
        ),
        grid_spec=pltpu.PrefetchScalarGridSpec(
            num_scalar_prefetch=1,
            grid=(),
            in_specs=[whole(), whole(), whole(), whole(), whole(), hbm()],
            out_specs=[hbm(), whole()],
            scratch_shapes=[
                pltpu.VMEM((count, PAD_ROWS, HEAD_DIM), jnp.bfloat16),
                pltpu.VMEM((count * group, PAD_ROWS), jnp.float32),
                pltpu.VMEM((count, group, HEAD_DIM), jnp.float32),
                pltpu.SemaphoreType.DMA((count,)),
                pltpu.SemaphoreType.DMA((count,)),
            ],
        ),
        compiler_params=pltpu.CompilerParams(vmem_limit_bytes=16 * 1024 * 1024),
        name="attend",
    )(sources, queries, keys, values, bias, out_weight, recv)


def spread_kernel(
    block_ref,
    page_hbm,
    length_hbm,
    count_hbm,
    order_hbm,
    keep_hbm,
    weight_hbm,
    cache_rows_hbm,
    send_hbm,
    rows_vmem,
    out_vmem,
    wide_vmem,
    order_vmem,
    keep_vmem,
    weight_vmem,
    spot_vmem,
    dest_vmem,
    page_smem,
    length_smem,
    count_smem,
    spot_smem,
    dest_smem,
    used_smem,
    free_smem,
    small_sem,
    load_sem,
    spot_sem,
    dest_sem,
    out_sem,
):
    count = keep_vmem.shape[0]
    group = 16
    pool_rows = cache_rows_hbm.shape[0]
    slots = send_hbm.shape[0] // ROUND_ONE
    relays = slots - count
    shift = relays.bit_length() - 1
    first = pl.multiple_of(block_ref[0] * count, count)
    small = [
        pltpu.make_async_copy(source, target, small_sem.at[n])
        for n, (source, target) in enumerate(
            [
                (keep_hbm.at[pl.ds(first, count)], keep_vmem),
                (count_hbm, count_smem),
                (page_hbm, page_smem),
                (order_hbm, order_vmem),
                (length_hbm, length_smem),
                (weight_hbm.at[pl.ds(first, count)], weight_vmem),
            ]
        )
    ]
    for copy in small:
        copy.start()
    load_rows = pltpu.make_async_copy(
        cache_rows_hbm, rows_vmem.at[pl.ds(0, pool_rows)], load_sem
    )
    load_rows.start()
    for copy in small:
        copy.wait()

    order = order_vmem[...]
    place = (
        lax.broadcasted_iota(jnp.int32, order.shape, 0) * order.shape[1]
        + lax.broadcasted_iota(jnp.int32, order.shape, 1)
    ) // count
    targets = [jnp.sum(jnp.where(order == first + i, place, 0)) for i in range(count)]

    keep = keep_vmem[...]
    slot_id = lax.broadcasted_iota(jnp.int32, keep.shape, 1)
    row_id = lax.broadcasted_iota(jnp.int32, keep.shape, 0)
    counts = jnp.zeros(keep.shape, jnp.int32)
    base = jnp.zeros(keep.shape, jnp.int32)
    target = jnp.zeros(keep.shape, jnp.int32)
    page_of = keep >> 6
    for i in range(count):
        here = row_id == i
        counts = jnp.where(here, count_smem[first + i], counts)
        target = jnp.where(here, targets[i], target)
        for j in range(PAGES):
            base = jnp.where(here & (page_of == j), page_smem[j, i] * PAGE, base)
    keep = jnp.where(slot_id < counts, keep, CAP)
    spot_vmem[...] = jnp.where(slot_id < counts, base + (keep & (PAGE - 1)), pool_rows)
    move_spots = pltpu.make_async_copy(spot_vmem, spot_smem, spot_sem)
    move_spots.start()

    for m in range(slots):
        used_smem[m] = 0
    for i in range(count):
        used_smem[targets[i]] = 1
    free = 0
    for m in range(slots):
        free_smem[free] = m
        free = free + 1 - used_smem[m]
    before = jnp.zeros(keep.shape, jnp.int32)
    for i in range(count):
        beyond = jnp.maximum(count_smem[first + i] + PAGES - ROUND_ONE, 0)
        before = before + jnp.where(target > targets[i], beyond, 0)
    entry = slot_id + PAGES
    ordinal = jnp.maximum(before + entry - ROUND_ONE, 0)
    turn = ordinal & (relays - 1)
    relay = jnp.zeros(keep.shape, jnp.int32)
    for j in range(relays):
        relay = jnp.where(turn == j, free_smem[j], relay)
    depth = jnp.minimum(ordinal >> shift, ROUND_ONE - 1)
    dest = jnp.where(
        entry < ROUND_ONE, target * ROUND_ONE + entry, relay * ROUND_ONE + depth
    )
    dest_vmem[...] = jnp.where(slot_id < counts, dest, slots * ROUND_ONE)
    move_dests = pltpu.make_async_copy(dest_vmem, dest_smem, dest_sem)
    move_dests.start()

    keep_cols = jnp.transpose(keep.astype(jnp.float32))
    lane_pos = lax.broadcasted_iota(jnp.int32, (KEPT, CAP), 1).astype(jnp.float32)
    spot = lax.broadcasted_iota(jnp.int32, (1, CAP), 1)
    factors = []
    for i in range(count):
        match = keep_cols[:, i : i + 1] == lane_pos
        kept = jnp.max(jnp.where(match, 1.0, 0.0), axis=0, keepdims=True)
        dropped = (spot < length_smem[first + i]) & (kept < 0.5)
        factors.append(jnp.where(dropped, weight_vmem[i : i + 1, :], 0.0))
    factors = jnp.concatenate(factors, axis=0).astype(jnp.bfloat16)
    repeat = (
        lax.broadcasted_iota(jnp.int32, (CAP, CAP * LANES), 1) >> 2
        == lax.broadcasted_iota(jnp.int32, (CAP, CAP * LANES), 0)
    )
    repeat = jnp.where(repeat, 1.0, 0.0).astype(jnp.bfloat16)
    wide_vmem[...] = jnp.dot(factors, repeat, preferred_element_type=jnp.float32)
    page_lanes = PAGE * LANES
    out_row = lax.broadcasted_iota(jnp.int32, (PAGES * LANES, page_lanes), 0)
    out_lane = lax.broadcasted_iota(jnp.int32, (PAGES * LANES, page_lanes), 1)
    same = (out_row & (LANES - 1)) == (out_lane & (LANES - 1))
    selectors = [jnp.where(same & (out_row >> 2 == j), 1.0, 0.0) for j in range(PAGES)]

    zero_rows = jnp.zeros((group, LANES, HEAD_DIM), jnp.bfloat16)
    rows_vmem[pl.ds(pool_rows, 8)] = zero_rows[:8]

    def clear(c, carry):
        for u in range(4):
            out_vmem[pl.ds(pl.multiple_of((c * 4 + u) * group, group), group)] = zero_rows
        return carry

    lax.fori_loop(0, slots * ROUND_ONE // (4 * group), clear, 0)
    move_spots.wait()
    move_dests.wait()
    load_rows.wait()
    for i in range(count):

        def gather(c, carry):
            picked = [rows_vmem[spot_smem[i, c * group + u]] for u in range(group)]
            for u in range(group):
                out_vmem[dest_smem[i, c * group + u]] = picked[u]
            return carry

        lax.fori_loop(0, (count_smem[first + i] + group - 1) >> 4, gather, 0)

    flat = rows_vmem.reshape(rows_vmem.shape[0] * LANES, HEAD_DIM)
    for i in range(count):
        merged = jnp.zeros((PAGES * LANES, HEAD_DIM), jnp.float32)
        for j in range(PAGES):
            wide = wide_vmem[i : i + 1, j * page_lanes : (j + 1) * page_lanes]
            start = pl.multiple_of(page_smem[j, i] * page_lanes, page_lanes)
            merged = merged + jnp.dot(
                (selectors[j] * wide).astype(jnp.bfloat16),
                flat[pl.ds(start, page_lanes)],
                preferred_element_type=jnp.float32,
            )
        out_vmem[pl.ds(targets[i] * ROUND_ONE, PAGES)] = merged.astype(jnp.bfloat16).reshape(
            PAGES, LANES, HEAD_DIM
        )
    out = pltpu.make_async_copy(out_vmem.at[pl.ds(0, slots * ROUND_ONE)], send_hbm, out_sem)
    out.start()
    out.wait()


def spread(block_index, page_table, lengths, counts, order, positions, weights, cache_pool, blocks):
    count = page_table.shape[0]
    pool = cache_pool.shape[0]
    view = cache_pool.reshape(pool, PAGE, 2, HEADS_HERE, HEAD_DIM).transpose(0, 1, 3, 2, 4)
    as_rows = view.reshape(pool * PAGE, LANES, HEAD_DIM)
    requests = order.shape[0]
    hbm = lambda: pl.BlockSpec(memory_space=pltpu.HBM)
    operands = [
        page_table.T,
        lengths,
        counts,
        order.reshape(requests // 128, 128),
        positions,
        weights,
        as_rows,
    ]
    operands = [pltpu.with_memory_space_constraint(x, pltpu.HBM) for x in operands]
    return pl.pallas_call(
        spread_kernel,
        out_shape=pltpu.HBM((blocks * ROUND_ONE, LANES, HEAD_DIM), jnp.bfloat16),
        grid_spec=pltpu.PrefetchScalarGridSpec(
            num_scalar_prefetch=1,
            grid=(),
            in_specs=[hbm() for _ in operands],
            out_specs=hbm(),
            scratch_shapes=[
                pltpu.VMEM((pool * PAGE + 8, LANES, HEAD_DIM), jnp.bfloat16),
                pltpu.VMEM((blocks * ROUND_ONE + 8, LANES, HEAD_DIM), jnp.bfloat16),
                pltpu.VMEM((count, CAP * LANES), jnp.float32),
                pltpu.VMEM((requests // 128, 128), jnp.int32),
                pltpu.VMEM((count, KEPT), jnp.int32),
                pltpu.VMEM((count, CAP), jnp.float32),
                pltpu.VMEM((count, KEPT), jnp.int32),
                pltpu.VMEM((count, KEPT), jnp.int32),
                pltpu.SMEM((PAGES, count), jnp.int32),
                pltpu.SMEM((requests,), jnp.int32),
                pltpu.SMEM((requests,), jnp.int32),
                pltpu.SMEM((count, KEPT), jnp.int32),
                pltpu.SMEM((count, KEPT), jnp.int32),
                pltpu.SMEM((blocks,), jnp.int32),
                pltpu.SMEM((blocks + 1,), jnp.int32),
                pltpu.SemaphoreType.DMA((6,)),
                pltpu.SemaphoreType.DMA(()),
                pltpu.SemaphoreType.DMA(()),
                pltpu.SemaphoreType.DMA(()),
                pltpu.SemaphoreType.DMA(()),
            ],
        ),
        compiler_params=pltpu.CompilerParams(vmem_limit_bytes=20 * 1024 * 1024),
        name="spread",
    )(jnp.reshape(block_index, (1,)), *operands)


def relay_kernel(held_ref, dest_ref, recv_ref, send_hbm, out_vmem, out_sem):
    slots = held_ref.shape[0]

    def source(s, carry):
        def forward(c, inner):
            start = s * ROUND_ONE + c * STEP
            picked = [recv_ref[start + u] for u in range(STEP)]
            for u in range(STEP):
                out_vmem[dest_ref[s, c * STEP + u]] = picked[u]
            return inner

        lax.fori_loop(0, lax.div(held_ref[s] + (STEP - 1), STEP), forward, 0)
        return carry

    lax.fori_loop(0, slots, source, 0)
    out = pltpu.make_async_copy(out_vmem.at[pl.ds(0, slots * ROUND_TWO)], send_hbm, out_sem)
    out.start()
    out.wait()


def forward_rows(held, dest, recv, blocks):
    return pl.pallas_call(
        relay_kernel,
        out_shape=pltpu.HBM((blocks * ROUND_TWO, LANES, HEAD_DIM), jnp.bfloat16),
        grid_spec=pltpu.PrefetchScalarGridSpec(
            num_scalar_prefetch=2,
            grid=(),
            in_specs=[pl.BlockSpec(memory_space=pltpu.VMEM)],
            out_specs=pl.BlockSpec(memory_space=pltpu.HBM),
            scratch_shapes=[
                pltpu.VMEM((blocks * ROUND_TWO + 8, LANES, HEAD_DIM), jnp.bfloat16),
                pltpu.SemaphoreType.DMA(()),
            ],
        ),
        compiler_params=pltpu.CompilerParams(vmem_limit_bytes=12 * 1024 * 1024),
        name="relay",
    )(held, dest, recv)


def gather_attend_kernel(
    source_ref,
    beyond_ref,
    place_ref,
    query_ref,
    key_ref,
    value_ref,
    bias_ref,
    weight_ref,
    direct_ref,
    relayed_ref,
    packed_hbm,
    share_ref,
    rows_vmem,
    score_vmem,
    attended_vmem,
    out_sem,
):
    count, group = query_ref.shape[:2]
    head = ROUND_ONE - PAGES
    zero_rows = jnp.zeros((8, LANES, HEAD_DIM), jnp.bfloat16)
    for r in range(count):
        for c in range(head, KEPT, 8):
            rows_vmem[pl.ds(r * SLOTS + min(c, KEPT - 8), 8)] = zero_rows
    for c in range((rows_vmem.shape[0] - count * SLOTS) // 8):
        rows_vmem[pl.ds(count * SLOTS + c * 8, 8)] = zero_rows
    scale = HEAD_DIM ** (-0.5)
    contract_last = (((1,), (1,)), ((), ()))
    own_score = (
        jnp.sum(
            query_ref[...].astype(jnp.float32) * key_ref[...].astype(jnp.float32),
            axis=-1,
            keepdims=True,
        )
        * scale
    ).reshape(count * group, 1)
    outs = [
        pltpu.make_async_copy(
            rows_vmem.at[pl.ds(r * SLOTS, SLOTS)],
            packed_hbm.at[pl.ds(r * SLOTS, SLOTS)],
            out_sem.at[r],
        )
        for r in range(count)
    ]
    for r in range(count):
        source = source_ref[r]
        beyond = beyond_ref[source]
        start = source * ROUND_ONE
        rows_vmem[pl.ds(r * SLOTS, head)] = direct_ref[pl.ds(start + PAGES, head)]
        rows_vmem[pl.ds(r * SLOTS + KEPT, PAGES)] = direct_ref[pl.ds(start, PAGES)]

        def place(c, carry):
            picked = [relayed_ref[place_ref[source, c * STEP + u]] for u in range(STEP)]
            for u in range(STEP):
                past = c * STEP + u >= beyond
                rows_vmem[r * SLOTS + head + c * STEP + u] = jnp.where(
                    past, zero_rows[0], picked[u]
                )
            return carry

        lax.fori_loop(0, lax.div(beyond + (STEP - 1), STEP), place, 0)
        outs[r].start()
    flat = rows_vmem.reshape(rows_vmem.shape[0] * LANES, HEAD_DIM)
    for r in range(count):
        scores = lax.dot_general(
            query_ref[r],
            flat[pl.ds(r * ROWS, PAD_ROWS)],
            contract_last,
            preferred_element_type=jnp.float32,
        )
        score_vmem[r * group : (r + 1) * group, :] = scores * scale + bias_ref[r]
    scores = score_vmem[...]
    highest = jnp.maximum(jnp.max(scores, axis=-1, keepdims=True), own_score)
    exponentials = jnp.exp(scores - highest)
    own_exp = jnp.exp(own_score - highest)
    denominator = jnp.sum(exponentials, axis=-1, keepdims=True) + own_exp
    probabilities = exponentials / denominator
    own_prob = (own_exp / denominator).astype(jnp.bfloat16).astype(jnp.float32)
    score_vmem[...] = pltpu.roll(probabilities, 1, axis=1)
    for r in range(count):
        moved = score_vmem[r * group : (r + 1) * group, :].astype(jnp.bfloat16)
        combined = jnp.dot(
            moved, flat[pl.ds(r * ROWS, PAD_ROWS)], preferred_element_type=jnp.float32
        )
        attended_vmem[r] = combined + own_prob[
            r * group : (r + 1) * group
        ] * value_ref[r].astype(jnp.float32)
    attended = jnp.concatenate(
        [attended_vmem[:, h, :] for h in range(HEADS_HERE)], axis=1
    ).astype(jnp.bfloat16)
    share = jnp.dot(attended, weight_ref[...], preferred_element_type=jnp.float32).astype(
        jnp.bfloat16
    )
    width = share_ref.shape[2]
    for e in range(share_ref.shape[0]):
        share_ref[e] = share[:, e * width : (e + 1) * width]
    for r in range(count):
        outs[r].wait()


def gather_attend(
    sources, beyond, places, queries, keys, values, bias, out_weight, direct, relayed, peers
):
    count, group = queries.shape[:2]
    width = out_weight.shape[1] // peers
    whole = lambda: pl.BlockSpec(memory_space=pltpu.VMEM)
    hbm = lambda: pl.BlockSpec(memory_space=pltpu.HBM)
    spare = -(-(PAD_ROWS - ROWS) // (8 * LANES)) * 8
    return pl.pallas_call(
        gather_attend_kernel,
        out_shape=(
            pltpu.HBM((count * SLOTS, LANES, HEAD_DIM), jnp.bfloat16),
            jax.ShapeDtypeStruct((peers, count, width), jnp.bfloat16),
        ),
        grid_spec=pltpu.PrefetchScalarGridSpec(
            num_scalar_prefetch=3,
            grid=(),
            in_specs=[whole() for _ in range(7)],
            out_specs=[hbm(), whole()],
            scratch_shapes=[
                pltpu.VMEM((count * SLOTS + spare, LANES, HEAD_DIM), jnp.bfloat16),
                pltpu.VMEM((count * group, PAD_ROWS), jnp.float32),
                pltpu.VMEM((count, group, HEAD_DIM), jnp.float32),
                pltpu.SemaphoreType.DMA((count,)),
            ],
        ),
        compiler_params=pltpu.CompilerParams(vmem_limit_bytes=16 * 1024 * 1024),
        name="gather_attend",
    )(
        sources,
        beyond,
        places,
        queries,
        keys,
        values,
        bias,
        out_weight,
        direct,
        relayed,
    )


def routes(request_order, retained_counts, block_index, blocks, rows_here):
    relays = blocks - rows_here
    shift = relays.bit_length() - 1
    ids = jnp.arange(request_order.shape[0], dtype=jnp.int32)
    line = jnp.arange(blocks, dtype=jnp.int32)
    target_of = jnp.sum(
        jnp.where(request_order[None, :] == ids[:, None], (ids // rows_here)[None, :], 0), axis=1
    ).reshape(blocks, rows_here)
    rows = retained_counts.reshape(blocks, rows_here) + PAGES
    sent = jnp.sum(
        jnp.where(target_of[:, :, None] == line[None, None, :], rows[:, :, None], 0), axis=1
    )
    free = sent == 0
    beyond = jnp.maximum(sent - ROUND_ONE, 0)
    lower = line[None, :] < line[:, None]
    prefix = lambda array: jnp.sum(jnp.where(lower[None], array[:, None, :], 0), axis=2)
    start = prefix(beyond)
    rank = prefix(free.astype(jnp.int32))
    total = jnp.sum(beyond, axis=1)
    until = lambda ordinal, turn: (ordinal - turn + (relays - 1)) >> shift
    above = lambda array: jnp.sum(jnp.where(lower[:, :, None], array[None], 0), axis=1)
    pick = lambda array: jnp.sum(jnp.where(line[None, :] == block_index, array, 0), axis=1)

    loads = jnp.sum(
        jnp.where(
            free[:, :, None],
            until((start + beyond)[:, None, :], rank[:, :, None])
            - until(start[:, None, :], rank[:, :, None]),
            0,
        ),
        axis=0,
    )
    fits = jnp.all(total <= ROUND_ONE * relays) & jnp.all(loads <= ROUND_TWO)

    turn = pick(rank)
    serves = pick(free.astype(jnp.int32)) > 0
    begin = until(start, turn[:, None])
    passed = jnp.where(serves[:, None], until(start + beyond, turn[:, None]) - begin, 0)
    shifted = line[None, :] * ROUND_TWO + above(passed) - begin
    depth = jnp.arange(64, dtype=jnp.int32)
    ordinal = depth[None, :] * relays + turn[:, None]
    inside = (ordinal[:, :, None] >= start[:, None, :]) & (
        ordinal[:, :, None] < (start + beyond)[:, None, :]
    )
    dest = jnp.sum(jnp.where(inside, shifted[:, None, :], 0), axis=2) + depth[None, :]
    limit = blocks * ROUND_TWO
    good = serves[:, None] & (ordinal < total[:, None]) & (depth < ROUND_ONE)[None, :]
    dest = jnp.where(good, jnp.clip(dest, 0, limit - 1), limit)
    held = jnp.where(serves, jnp.clip(until(total, turn), 0, ROUND_ONE), 0)

    mine_start = pick(start)
    mine_beyond = pick(beyond)
    begin = until(mine_start[:, None], rank)
    passed = jnp.where(free, until((mine_start + mine_beyond)[:, None], rank) - begin, 0)
    shifted = line[None, :] * ROUND_TWO + above(passed) - begin
    entry = jnp.arange(128, dtype=jnp.int32)
    ordinal = mine_start[:, None] + entry[None, :]
    chosen = free[:, None, :] & (rank[:, None, :] == (ordinal & (relays - 1))[:, :, None])
    places = jnp.sum(jnp.where(chosen, shifted[:, None, :], 0), axis=2) + (ordinal >> shift)
    places = jnp.where(
        entry[None, :] < mine_beyond[:, None], jnp.clip(places, 0, limit - 1), 0
    )
    return fits, held, dest, mine_beyond, places


def local(
    hidden_in,
    qkv_weight,
    out_weight,
    cache_pool,
    page_table,
    request_order,
    request_lengths,
    retained_counts,
    retained_positions,
    blended_weight,
):
    rows_here = hidden_in.shape[0]
    head_width = qkv_weight.shape[2]
    heads_here = head_width // HEAD_DIM
    blocks = lax.axis_size("blk")
    peers = lax.axis_size("head")
    block_index = lax.axis_index("blk")
    first = block_index * rows_here
    slot_index = jnp.arange(KEPT, dtype=jnp.int32)
    take = lambda array: lax.dynamic_slice_in_dim(array, first, rows_here, 0)

    source_arguments = (
        block_index,
        page_table,
        request_lengths,
        retained_counts,
        request_order,
        retained_positions,
        blended_weight,
        cache_pool,
        blocks,
    )

    def exchange(rows):
        return lax.all_to_all(
            rows.reshape(blocks, -1, HEAD_DIM), "blk", split_axis=0, concat_axis=0, tiled=True
        )

    direct = exchange(spread(*source_arguments)).reshape(-1, LANES, HEAD_DIM)
    fits, held, dest, beyond, places = routes(
        request_order, retained_counts, block_index, blocks, rows_here
    )

    old_ids = take(request_order)
    sources = old_ids // rows_here
    lengths = request_lengths[old_ids]
    counts = retained_counts[old_ids]
    keep = jnp.where(slot_index[None, :] < counts[:, None], retained_positions[old_ids], CAP)
    spots = jnp.arange(CAP, dtype=jnp.int32)
    dropped = (spots[None, :] < lengths[:, None]) & jnp.logical_not(
        jnp.any(keep[:, :, None] == spots[None, None, :], axis=1)
    )
    dropped_weight = jnp.where(dropped, blended_weight[old_ids], 0.0)
    dropped_mass = jnp.log(1.0 + jnp.sum(dropped_weight.reshape(rows_here, PAGES, PAGE), axis=2))
    page_start = jnp.arange(PAGES, dtype=jnp.int32) * PAGE
    bias_slots = jnp.concatenate(
        [
            jnp.where(slot_index[None, :] < counts[:, None], 0.0, NEG),
            jnp.where(page_start[None, :] < lengths[:, None], dropped_mass, NEG),
        ],
        axis=1,
    )
    columns = jnp.arange(ROWS, dtype=jnp.int32) % LANES
    head_rows = jnp.arange(8, dtype=jnp.int32)
    bias = jnp.where(
        columns[None, None, :] == 2 * head_rows[None, :, None],
        jnp.repeat(bias_slots, LANES, axis=1)[:, None, :],
        NEG,
    )
    bias = jnp.pad(bias, ((0, 0), (0, 0), (0, PAD_ROWS - ROWS)), constant_values=NEG)

    gathered = lax.all_gather(hidden_in, "head", axis=1, tiled=True)
    held, dest, beyond, places, sources, bias, fits, gathered = lax.optimization_barrier(
        (held, dest, beyond, places, sources, bias, fits, gathered)
    )
    relayed = exchange(forward_rows(held, dest, direct, blocks)).reshape(-1, LANES, HEAD_DIM)

    normed = layer_norm(gathered.astype(jnp.float32)).astype(jnp.bfloat16)
    project = lambda index: jnp.dot(
        normed, qkv_weight[:, index], preferred_element_type=jnp.float32
    ).reshape(rows_here, heads_here, HEAD_DIM)
    pad_heads = lambda array: jnp.pad(
        array.astype(jnp.bfloat16), ((0, 0), (0, 8 - heads_here), (0, 0))
    )
    queries = pad_heads(rotate(project(0), lengths))
    new_keys = pad_heads(rotate(project(1), lengths))
    new_values = pad_heads(project(2))

    def whole_shape(packed):
        return (
            packed.reshape(rows_here, SLOTS, heads_here, 2, HEAD_DIM)
            .transpose(0, 1, 3, 2, 4)
            .reshape(rows_here, SLOTS, 2, head_width)
        )

    def two_rounds():
        packed, share = gather_attend(
            sources,
            beyond,
            places,
            queries,
            new_keys,
            new_values,
            bias,
            out_weight,
            direct,
            relayed,
            peers,
        )
        return whole_shape(packed), share

    def one_round():
        arrived = exchange(pack(*source_arguments))
        packed, share = attend(
            sources, queries, new_keys, new_values, bias, out_weight, arrived, peers
        )
        return whole_shape(packed), share

    packed_cache, share = lax.cond(fits, two_rounds, one_round)
    parts = lax.all_to_all(share, "head", split_axis=0, concat_axis=0, tiled=True)
    summed = jnp.sum(parts.astype(jnp.float32), axis=0)
    hidden_out = (hidden_in.astype(jnp.float32) + summed).astype(jnp.bfloat16)
    return (hidden_out, packed_cache)


def solution(mesh):
    return jax.shard_map(
        local,
        mesh=mesh,
        in_specs=(
            P("blk", "head"),
            P(None, None, "head"),
            P("head", None),
            P("blk", None, None, "head"),
            P("blk", None),
            P(),
            P(),
            P(),
            P(),
            P(),
        ),
        out_specs=(P("blk", "head"), P("blk", None, None, "head")),
        check_vma=False,
    )
```

```python
import functools

import jax
import jax.numpy as jnp
from jax import lax
from jax.experimental import pallas as pl
from jax.experimental.pallas import tpu as pltpu
from jax.sharding import PartitionSpec as P

HEAD_DIM = 128
PAGE = 64
PAGES = 4
CAP = 256
KEPT = 128
SLOTS = 132
HEADS_HERE = 2
LANES = HEADS_HERE * 2
ROWS = SLOTS * LANES
PAD_ROWS = 640
NEG = -1e30
ROUND_ONE = 54
ROUND_TWO = 36
STEP = 6

epsilon = 1e-05


def layer_norm(hidden):
    average = jnp.mean(hidden, axis=-1, keepdims=True)
    centered = hidden - average
    variance = jnp.mean(centered * centered, axis=-1, keepdims=True)
    return centered * lax.rsqrt(variance + epsilon)


def rotate(vectors, positions):
    half_dim = vectors.shape[-1] // 2
    inverse_freq = 10000.0 ** (-jnp.arange(half_dim, dtype=jnp.float32) / half_dim)
    angles = positions.astype(jnp.float32)[:, None, None] * inverse_freq
    cosine = jnp.cos(angles)
    sine_part = jnp.sin(angles)
    first_half = vectors[..., :half_dim]
    second_half = vectors[..., half_dim:]
    return jnp.concatenate(
        [
            first_half * cosine - second_half * sine_part,
            second_half * cosine + first_half * sine_part,
        ],
        axis=-1,
    )


def pack_kernel(
    block_ref,
    page_hbm,
    length_hbm,
    count_hbm,
    order_hbm,
    keep_hbm,
    weight_hbm,
    cache_rows_hbm,
    cache_flat_hbm,
    send_hbm,
    rows_vmem,
    flat_vmem,
    out_vmem,
    wide_vmem,
    order_vmem,
    keep_vmem,
    weight_vmem,
    spot_vmem,
    page_smem,
    length_smem,
    count_smem,
    spot_smem,
    small_sem,
    load_sem,
    spot_sem,
    out_sem,
):
    count = keep_vmem.shape[0]
    group = 16
    pool_rows = cache_rows_hbm.shape[0]
    first = pl.multiple_of(block_ref[0] * count, count)
    small = [
        pltpu.make_async_copy(source, target, small_sem.at[n])
        for n, (source, target) in enumerate(
            [
                (keep_hbm.at[pl.ds(first, count)], keep_vmem),
                (count_hbm, count_smem),
                (page_hbm, page_smem),
                (order_hbm, order_vmem),
                (length_hbm, length_smem),
                (weight_hbm.at[pl.ds(first, count)], weight_vmem),
            ]
        )
    ]
    for copy in small:
        copy.start()
    load_rows = pltpu.make_async_copy(
        cache_rows_hbm, rows_vmem.at[pl.ds(0, pool_rows)], load_sem.at[0]
    )
    load_flat = pltpu.make_async_copy(cache_flat_hbm, flat_vmem, load_sem.at[1])
    load_rows.start()
    for copy in small:
        copy.wait()
    load_flat.start()

    keep = keep_vmem[...]
    slot_id = lax.broadcasted_iota(jnp.int32, keep.shape, 1)
    row_id = lax.broadcasted_iota(jnp.int32, keep.shape, 0)
    counts = jnp.zeros(keep.shape, jnp.int32)
    base = jnp.zeros(keep.shape, jnp.int32)
    page_of = keep >> 6
    for i in range(count):
        here = row_id == i
        counts = jnp.where(here, count_smem[first + i], counts)
        for j in range(PAGES):
            base = jnp.where(here & (page_of == j), page_smem[j, i] * PAGE, base)
    keep = jnp.where(slot_id < counts, keep, CAP)
    spot_vmem[...] = jnp.where(slot_id < counts, base + (keep & (PAGE - 1)), pool_rows)
    move_spots = pltpu.make_async_copy(spot_vmem, spot_smem, spot_sem)
    move_spots.start()

    order = order_vmem[...]
    place = (
        lax.broadcasted_iota(jnp.int32, order.shape, 0) * order.shape[1]
        + lax.broadcasted_iota(jnp.int32, order.shape, 1)
    ) // count
    targets = [jnp.sum(jnp.where(order == first + i, place, 0)) for i in range(count)]

    keep_cols = jnp.transpose(keep.astype(jnp.float32))
    lane_pos = lax.broadcasted_iota(jnp.int32, (KEPT, CAP), 1).astype(jnp.float32)
    spot = lax.broadcasted_iota(jnp.int32, (1, CAP), 1)
    factors = []
    for i in range(count):
        match = keep_cols[:, i : i + 1] == lane_pos
        kept = jnp.max(jnp.where(match, 1.0, 0.0), axis=0, keepdims=True)
        dropped = (spot < length_smem[first + i]) & (kept < 0.5)
        factors.append(jnp.where(dropped, weight_vmem[i : i + 1, :], 0.0))
    factors = jnp.concatenate(factors, axis=0).astype(jnp.bfloat16)
    spread = (
        lax.broadcasted_iota(jnp.int32, (CAP, CAP * LANES), 1) >> 2
        == lax.broadcasted_iota(jnp.int32, (CAP, CAP * LANES), 0)
    )
    spread = jnp.where(spread, 1.0, 0.0).astype(jnp.bfloat16)
    wide_vmem[...] = jnp.dot(factors, spread, preferred_element_type=jnp.float32)
    page_lanes = PAGE * LANES
    out_row = lax.broadcasted_iota(jnp.int32, (PAGES * LANES, page_lanes), 0)
    out_lane = lax.broadcasted_iota(jnp.int32, (PAGES * LANES, page_lanes), 1)
    same = (out_row & (LANES - 1)) == (out_lane & (LANES - 1))
    selectors = [jnp.where(same & (out_row >> 2 == j), 1.0, 0.0) for j in range(PAGES)]

    zero_rows = jnp.zeros((group, LANES, HEAD_DIM), jnp.bfloat16)
    rows_vmem[pool_rows] = zero_rows[0]

    def clear(c, carry):
        for i in range(count):
            out_vmem[i, pl.ds(pl.multiple_of(c * group, group), group)] = zero_rows
        return carry

    lax.fori_loop(0, KEPT // group, clear, 0)
    move_spots.wait()
    load_rows.wait()
    for i in range(count):

        def gather(c, carry):
            picked = [rows_vmem[spot_smem[i, c * group + u]] for u in range(group)]
            for u in range(group):
                out_vmem[i, c * group + u] = picked[u]
            return carry

        full = (count_smem[first + i] + group - 1) >> 4
        lax.fori_loop(0, full, gather, 0)

    copies = [
        pltpu.make_async_copy(out_vmem.at[i], send_hbm.at[targets[i]], out_sem.at[i])
        for i in range(count)
    ]
    load_flat.wait()
    for i in range(count):
        merged = jnp.zeros((PAGES * LANES, HEAD_DIM), jnp.float32)
        for j in range(PAGES):
            wide = wide_vmem[i : i + 1, j * page_lanes : (j + 1) * page_lanes]
            merged = merged + jnp.dot(
                (selectors[j] * wide).astype(jnp.bfloat16),
                flat_vmem[page_smem[j, i]],
                preferred_element_type=jnp.float32,
            )
        out_vmem[i, pl.ds(KEPT, PAGES)] = merged.astype(jnp.bfloat16).reshape(
            PAGES, LANES, HEAD_DIM
        )
        copies[i].start()
    for copy in copies:
        copy.wait()


def pack(block_index, page_table, lengths, counts, order, positions, weights, cache_pool, blocks):
    count = page_table.shape[0]
    pool = cache_pool.shape[0]
    view = cache_pool.reshape(pool, PAGE, 2, HEADS_HERE, HEAD_DIM).transpose(0, 1, 3, 2, 4)
    as_rows = view.reshape(pool * PAGE, LANES, HEAD_DIM)
    as_flat = view.reshape(pool, PAGE * LANES, HEAD_DIM)
    requests = order.shape[0]
    hbm = lambda: pl.BlockSpec(memory_space=pltpu.HBM)
    operands = [
        page_table.T,
        lengths,
        counts,
        order.reshape(requests // 128, 128),
        positions,
        weights,
        as_rows,
        as_flat,
    ]
    operands = [pltpu.with_memory_space_constraint(x, pltpu.HBM) for x in operands]
    return pl.pallas_call(
        pack_kernel,
        out_shape=pltpu.HBM((blocks, SLOTS, LANES, HEAD_DIM), jnp.bfloat16),
        grid_spec=pltpu.PrefetchScalarGridSpec(
            num_scalar_prefetch=1,
            grid=(),
            in_specs=[hbm() for _ in operands],
            out_specs=hbm(),
            scratch_shapes=[
                pltpu.VMEM((pool * PAGE + 1, LANES, HEAD_DIM), jnp.bfloat16),
                pltpu.VMEM((pool, PAGE * LANES, HEAD_DIM), jnp.bfloat16),
                pltpu.VMEM((count, SLOTS, LANES, HEAD_DIM), jnp.bfloat16),
                pltpu.VMEM((count, CAP * LANES), jnp.float32),
                pltpu.VMEM((requests // 128, 128), jnp.int32),
                pltpu.VMEM((count, KEPT), jnp.int32),
                pltpu.VMEM((count, CAP), jnp.float32),
                pltpu.VMEM((count, KEPT), jnp.int32),
                pltpu.SMEM((PAGES, count), jnp.int32),
                pltpu.SMEM((requests,), jnp.int32),
                pltpu.SMEM((requests,), jnp.int32),
                pltpu.SMEM((count, KEPT), jnp.int32),
                pltpu.SemaphoreType.DMA((6,)),
                pltpu.SemaphoreType.DMA((2,)),
                pltpu.SemaphoreType.DMA(()),
                pltpu.SemaphoreType.DMA((count,)),
            ],
        ),
        compiler_params=pltpu.CompilerParams(vmem_limit_bytes=24 * 1024 * 1024),
        name="pack",
    )(jnp.reshape(block_index, (1,)), *operands)


def attend_kernel(
    source_ref,
    query_ref,
    key_ref,
    value_ref,
    bias_ref,
    weight_ref,
    recv_hbm,
    packed_hbm,
    share_ref,
    rows_vmem,
    score_vmem,
    attended_vmem,
    in_sem,
    out_sem,
):
    count = query_ref.shape[0]
    group = query_ref.shape[1]
    ins = [
        pltpu.make_async_copy(
            recv_hbm.at[source_ref[r]], rows_vmem.at[r, pl.ds(0, ROWS)], in_sem.at[r]
        )
        for r in range(count)
    ]
    outs = [
        pltpu.make_async_copy(rows_vmem.at[r, pl.ds(0, ROWS)], packed_hbm.at[r], out_sem.at[r])
        for r in range(count)
    ]
    for r in range(count):
        ins[r].start()
    for r in range(count):
        rows_vmem[r, pl.ds(ROWS, PAD_ROWS - ROWS)] = jnp.zeros(
            (PAD_ROWS - ROWS, HEAD_DIM), jnp.bfloat16
        )
    scale = HEAD_DIM ** (-0.5)
    contract_last = (((1,), (1,)), ((), ()))
    own_score = (
        jnp.sum(
            query_ref[...].astype(jnp.float32) * key_ref[...].astype(jnp.float32),
            axis=-1,
            keepdims=True,
        )
        * scale
    ).reshape(count * group, 1)
    for r in range(count):
        ins[r].wait()
        outs[r].start()
        scores = lax.dot_general(
            query_ref[r], rows_vmem[r], contract_last, preferred_element_type=jnp.float32
        )
        score_vmem[r * group : (r + 1) * group, :] = scores * scale + bias_ref[r]
    scores = score_vmem[...]
    highest = jnp.maximum(jnp.max(scores, axis=-1, keepdims=True), own_score)
    exponentials = jnp.exp(scores - highest)
    own_exp = jnp.exp(own_score - highest)
    denominator = jnp.sum(exponentials, axis=-1, keepdims=True) + own_exp
    probabilities = exponentials / denominator
    own_prob = (own_exp / denominator).astype(jnp.bfloat16).astype(jnp.float32)
    score_vmem[...] = pltpu.roll(probabilities, 1, axis=1)
    for r in range(count):
        moved = score_vmem[r * group : (r + 1) * group, :].astype(jnp.bfloat16)
        combined = jnp.dot(moved, rows_vmem[r], preferred_element_type=jnp.float32)
        attended_vmem[r] = combined + own_prob[
            r * group : (r + 1) * group
        ] * value_ref[r].astype(jnp.float32)
    attended = jnp.concatenate(
        [attended_vmem[:, h, :] for h in range(HEADS_HERE)], axis=1
    ).astype(jnp.bfloat16)
    share = jnp.dot(attended, weight_ref[...], preferred_element_type=jnp.float32).astype(
        jnp.bfloat16
    )
    width = share_ref.shape[2]
    for e in range(share_ref.shape[0]):
        share_ref[e] = share[:, e * width : (e + 1) * width]
    for r in range(count):
        outs[r].wait()


def attend(sources, queries, keys, values, bias, out_weight, recv, peers):
    count, group = queries.shape[:2]
    width = out_weight.shape[1] // peers
    whole = lambda: pl.BlockSpec(memory_space=pltpu.VMEM)
    hbm = lambda: pl.BlockSpec(memory_space=pltpu.HBM)
    return pl.pallas_call(
        attend_kernel,
        out_shape=(
            pltpu.HBM((count, ROWS, HEAD_DIM), jnp.bfloat16),
            jax.ShapeDtypeStruct((peers, count, width), jnp.bfloat16),
        ),
        grid_spec=pltpu.PrefetchScalarGridSpec(
            num_scalar_prefetch=1,
            grid=(),
            in_specs=[whole(), whole(), whole(), whole(), whole(), hbm()],
            out_specs=[hbm(), whole()],
            scratch_shapes=[
                pltpu.VMEM((count, PAD_ROWS, HEAD_DIM), jnp.bfloat16),
                pltpu.VMEM((count * group, PAD_ROWS), jnp.float32),
                pltpu.VMEM((count, group, HEAD_DIM), jnp.float32),
                pltpu.SemaphoreType.DMA((count,)),
                pltpu.SemaphoreType.DMA((count,)),
            ],
        ),
        compiler_params=pltpu.CompilerParams(vmem_limit_bytes=16 * 1024 * 1024),
        name="attend",
    )(sources, queries, keys, values, bias, out_weight, recv)


def spread_kernel(
    block_ref,
    page_hbm,
    length_hbm,
    count_hbm,
    order_hbm,
    keep_hbm,
    weight_hbm,
    cache_rows_hbm,
    send_hbm,
    rows_vmem,
    out_vmem,
    wide_vmem,
    order_vmem,
    keep_vmem,
    weight_vmem,
    spot_vmem,
    dest_vmem,
    page_smem,
    length_smem,
    count_smem,
    spot_smem,
    dest_smem,
    used_smem,
    free_smem,
    small_sem,
    load_sem,
    spot_sem,
    dest_sem,
    out_sem,
):
    count = keep_vmem.shape[0]
    group = 16
    pool_rows = cache_rows_hbm.shape[0]
    slots = send_hbm.shape[0] // ROUND_ONE
    relays = slots - count
    shift = relays.bit_length() - 1
    first = pl.multiple_of(block_ref[0] * count, count)
    small = [
        pltpu.make_async_copy(source, target, small_sem.at[n])
        for n, (source, target) in enumerate(
            [
                (keep_hbm.at[pl.ds(first, count)], keep_vmem),
                (count_hbm, count_smem),
                (page_hbm, page_smem),
                (order_hbm, order_vmem),
                (length_hbm, length_smem),
                (weight_hbm.at[pl.ds(first, count)], weight_vmem),
            ]
        )
    ]
    for copy in small:
        copy.start()
    load_rows = pltpu.make_async_copy(
        cache_rows_hbm, rows_vmem.at[pl.ds(0, pool_rows)], load_sem
    )
    load_rows.start()
    for copy in small:
        copy.wait()

    order = order_vmem[...]
    place = (
        lax.broadcasted_iota(jnp.int32, order.shape, 0) * order.shape[1]
        + lax.broadcasted_iota(jnp.int32, order.shape, 1)
    ) // count
    targets = [jnp.sum(jnp.where(order == first + i, place, 0)) for i in range(count)]

    keep = keep_vmem[...]
    slot_id = lax.broadcasted_iota(jnp.int32, keep.shape, 1)
    row_id = lax.broadcasted_iota(jnp.int32, keep.shape, 0)
    counts = jnp.zeros(keep.shape, jnp.int32)
    base = jnp.zeros(keep.shape, jnp.int32)
    target = jnp.zeros(keep.shape, jnp.int32)
    page_of = keep >> 6
    for i in range(count):
        here = row_id == i
        counts = jnp.where(here, count_smem[first + i], counts)
        target = jnp.where(here, targets[i], target)
        for j in range(PAGES):
            base = jnp.where(here & (page_of == j), page_smem[j, i] * PAGE, base)
    keep = jnp.where(slot_id < counts, keep, CAP)
    spot_vmem[...] = jnp.where(slot_id < counts, base + (keep & (PAGE - 1)), pool_rows)
    move_spots = pltpu.make_async_copy(spot_vmem, spot_smem, spot_sem)
    move_spots.start()

    for m in range(slots):
        used_smem[m] = 0
    for i in range(count):
        used_smem[targets[i]] = 1
    free = 0
    for m in range(slots):
        free_smem[free] = m
        free = free + 1 - used_smem[m]
    before = jnp.zeros(keep.shape, jnp.int32)
    for i in range(count):
        beyond = jnp.maximum(count_smem[first + i] + PAGES - ROUND_ONE, 0)
        before = before + jnp.where(target > targets[i], beyond, 0)
    entry = slot_id + PAGES
    ordinal = jnp.maximum(before + entry - ROUND_ONE, 0)
    turn = ordinal & (relays - 1)
    relay = jnp.zeros(keep.shape, jnp.int32)
    for j in range(relays):
        relay = jnp.where(turn == j, free_smem[j], relay)
    depth = jnp.minimum(ordinal >> shift, ROUND_ONE - 1)
    dest = jnp.where(
        entry < ROUND_ONE, target * ROUND_ONE + entry, relay * ROUND_ONE + depth
    )
    dest_vmem[...] = jnp.where(slot_id < counts, dest, slots * ROUND_ONE)
    move_dests = pltpu.make_async_copy(dest_vmem, dest_smem, dest_sem)
    move_dests.start()

    keep_cols = jnp.transpose(keep.astype(jnp.float32))
    lane_pos = lax.broadcasted_iota(jnp.int32, (KEPT, CAP), 1).astype(jnp.float32)
    spot = lax.broadcasted_iota(jnp.int32, (1, CAP), 1)
    factors = []
    for i in range(count):
        match = keep_cols[:, i : i + 1] == lane_pos
        kept = jnp.max(jnp.where(match, 1.0, 0.0), axis=0, keepdims=True)
        dropped = (spot < length_smem[first + i]) & (kept < 0.5)
        factors.append(jnp.where(dropped, weight_vmem[i : i + 1, :], 0.0))
    factors = jnp.concatenate(factors, axis=0).astype(jnp.bfloat16)
    repeat = (
        lax.broadcasted_iota(jnp.int32, (CAP, CAP * LANES), 1) >> 2
        == lax.broadcasted_iota(jnp.int32, (CAP, CAP * LANES), 0)
    )
    repeat = jnp.where(repeat, 1.0, 0.0).astype(jnp.bfloat16)
    wide_vmem[...] = jnp.dot(factors, repeat, preferred_element_type=jnp.float32)
    page_lanes = PAGE * LANES
    out_row = lax.broadcasted_iota(jnp.int32, (PAGES * LANES, page_lanes), 0)
    out_lane = lax.broadcasted_iota(jnp.int32, (PAGES * LANES, page_lanes), 1)
    same = (out_row & (LANES - 1)) == (out_lane & (LANES - 1))
    selectors = [jnp.where(same & (out_row >> 2 == j), 1.0, 0.0) for j in range(PAGES)]

    zero_rows = jnp.zeros((group, LANES, HEAD_DIM), jnp.bfloat16)
    rows_vmem[pl.ds(pool_rows, 8)] = zero_rows[:8]

    def clear(c, carry):
        for u in range(4):
            out_vmem[pl.ds(pl.multiple_of((c * 4 + u) * group, group), group)] = zero_rows
        return carry

    lax.fori_loop(0, slots * ROUND_ONE // (4 * group), clear, 0)
    move_spots.wait()
    move_dests.wait()
    load_rows.wait()
    straight = (ROUND_ONE - PAGES) // group
    for i in range(count):
        slot = targets[i] * ROUND_ONE + PAGES
        full = (count_smem[first + i] + group - 1) >> 4

        def gather(c):
            picked = [rows_vmem[spot_smem[i, c * group + u]] for u in range(group)]
            for u in range(group):
                out_vmem[slot + c * group + u] = picked[u]

        def scatter(c):
            picked = [rows_vmem[spot_smem[i, c * group + u]] for u in range(group)]
            for u in range(group):
                out_vmem[dest_smem[i, c * group + u]] = picked[u]

        for c in range(straight):
            gather(c)
        for c in range(straight, KEPT // group):
            pl.when(c < full)(functools.partial(scatter, c))

    flat = rows_vmem.reshape(rows_vmem.shape[0] * LANES, HEAD_DIM)
    for i in range(count):
        merged = jnp.zeros((PAGES * LANES, HEAD_DIM), jnp.float32)
        for j in range(PAGES):
            wide = wide_vmem[i : i + 1, j * page_lanes : (j + 1) * page_lanes]
            start = pl.multiple_of(page_smem[j, i] * page_lanes, page_lanes)
            merged = merged + jnp.dot(
                (selectors[j] * wide).astype(jnp.bfloat16),
                flat[pl.ds(start, page_lanes)],
                preferred_element_type=jnp.float32,
            )
        out_vmem[pl.ds(targets[i] * ROUND_ONE, PAGES)] = merged.astype(jnp.bfloat16).reshape(
            PAGES, LANES, HEAD_DIM
        )
    out = pltpu.make_async_copy(out_vmem.at[pl.ds(0, slots * ROUND_ONE)], send_hbm, out_sem)
    out.start()
    out.wait()


def spread(block_index, page_table, lengths, counts, order, positions, weights, cache_pool, blocks):
    count = page_table.shape[0]
    pool = cache_pool.shape[0]
    view = cache_pool.reshape(pool, PAGE, 2, HEADS_HERE, HEAD_DIM).transpose(0, 1, 3, 2, 4)
    as_rows = view.reshape(pool * PAGE, LANES, HEAD_DIM)
    requests = order.shape[0]
    hbm = lambda: pl.BlockSpec(memory_space=pltpu.HBM)
    operands = [
        page_table.T,
        lengths,
        counts,
        order.reshape(requests // 128, 128),
        positions,
        weights,
        as_rows,
    ]
    operands = [pltpu.with_memory_space_constraint(x, pltpu.HBM) for x in operands]
    return pl.pallas_call(
        spread_kernel,
        out_shape=pltpu.HBM((blocks * ROUND_ONE, LANES, HEAD_DIM), jnp.bfloat16),
        grid_spec=pltpu.PrefetchScalarGridSpec(
            num_scalar_prefetch=1,
            grid=(),
            in_specs=[hbm() for _ in operands],
            out_specs=hbm(),
            scratch_shapes=[
                pltpu.VMEM((pool * PAGE + 8, LANES, HEAD_DIM), jnp.bfloat16),
                pltpu.VMEM((blocks * ROUND_ONE + 8, LANES, HEAD_DIM), jnp.bfloat16),
                pltpu.VMEM((count, CAP * LANES), jnp.float32),
                pltpu.VMEM((requests // 128, 128), jnp.int32),
                pltpu.VMEM((count, KEPT), jnp.int32),
                pltpu.VMEM((count, CAP), jnp.float32),
                pltpu.VMEM((count, KEPT), jnp.int32),
                pltpu.VMEM((count, KEPT), jnp.int32),
                pltpu.SMEM((PAGES, count), jnp.int32),
                pltpu.SMEM((requests,), jnp.int32),
                pltpu.SMEM((requests,), jnp.int32),
                pltpu.SMEM((count, KEPT), jnp.int32),
                pltpu.SMEM((count, KEPT), jnp.int32),
                pltpu.SMEM((blocks,), jnp.int32),
                pltpu.SMEM((blocks + 1,), jnp.int32),
                pltpu.SemaphoreType.DMA((6,)),
                pltpu.SemaphoreType.DMA(()),
                pltpu.SemaphoreType.DMA(()),
                pltpu.SemaphoreType.DMA(()),
                pltpu.SemaphoreType.DMA(()),
            ],
        ),
        compiler_params=pltpu.CompilerParams(vmem_limit_bytes=20 * 1024 * 1024),
        name="spread",
    )(jnp.reshape(block_index, (1,)), *operands)


def relay_kernel(held_ref, dest_ref, recv_ref, send_hbm, out_vmem, out_sem):
    slots = held_ref.shape[0]

    for s in range(slots):
        held = held_ref[s]

        def forward(c):
            start = s * ROUND_ONE + c * STEP
            picked = [recv_ref[start + u] for u in range(STEP)]
            for u in range(STEP):
                out_vmem[dest_ref[s, c * STEP + u]] = picked[u]

        @pl.when(held > 0)
        def _():
            for c in range(3):
                forward(c)
            for c in range(3, ROUND_ONE // STEP):
                pl.when(c * STEP < held)(functools.partial(forward, c))

    out = pltpu.make_async_copy(out_vmem.at[pl.ds(0, slots * ROUND_TWO)], send_hbm, out_sem)
    out.start()
    out.wait()


def forward_rows(held, dest, recv, blocks):
    return pl.pallas_call(
        relay_kernel,
        out_shape=pltpu.HBM((blocks * ROUND_TWO, LANES, HEAD_DIM), jnp.bfloat16),
        grid_spec=pltpu.PrefetchScalarGridSpec(
            num_scalar_prefetch=2,
            grid=(),
            in_specs=[pl.BlockSpec(memory_space=pltpu.VMEM)],
            out_specs=pl.BlockSpec(memory_space=pltpu.HBM),
            scratch_shapes=[
                pltpu.VMEM((blocks * ROUND_TWO + 8, LANES, HEAD_DIM), jnp.bfloat16),
                pltpu.SemaphoreType.DMA(()),
            ],
        ),
        compiler_params=pltpu.CompilerParams(vmem_limit_bytes=12 * 1024 * 1024),
        name="relay",
    )(held, dest, recv)


def gather_attend_kernel(
    source_ref,
    beyond_ref,
    place_ref,
    query_ref,
    key_ref,
    value_ref,
    bias_ref,
    weight_ref,
    direct_ref,
    relayed_ref,
    packed_hbm,
    share_ref,
    rows_vmem,
    score_vmem,
    attended_vmem,
    out_sem,
):
    count, group = query_ref.shape[:2]
    head = ROUND_ONE - PAGES
    zero_rows = jnp.zeros((8, LANES, HEAD_DIM), jnp.bfloat16)
    for r in range(count):
        for c in range(head, KEPT, 8):
            rows_vmem[pl.ds(r * SLOTS + min(c, KEPT - 8), 8)] = zero_rows
    for c in range((rows_vmem.shape[0] - count * SLOTS) // 8):
        rows_vmem[pl.ds(count * SLOTS + c * 8, 8)] = zero_rows
    scale = HEAD_DIM ** (-0.5)
    contract_last = (((1,), (1,)), ((), ()))
    own_score = (
        jnp.sum(
            query_ref[...].astype(jnp.float32) * key_ref[...].astype(jnp.float32),
            axis=-1,
            keepdims=True,
        )
        * scale
    ).reshape(count * group, 1)
    outs = [
        pltpu.make_async_copy(
            rows_vmem.at[pl.ds(r * SLOTS, SLOTS)],
            packed_hbm.at[pl.ds(r * SLOTS, SLOTS)],
            out_sem.at[r],
        )
        for r in range(count)
    ]
    for r in range(count):
        source = source_ref[r]
        beyond = beyond_ref[source]
        start = source * ROUND_ONE
        rows_vmem[pl.ds(r * SLOTS, head)] = direct_ref[pl.ds(start + PAGES, head)]
        rows_vmem[pl.ds(r * SLOTS + KEPT, PAGES)] = direct_ref[pl.ds(start, PAGES)]

        def place(c):
            picked = [relayed_ref[place_ref[source, c * STEP + u]] for u in range(STEP)]
            for u in range(STEP):
                past = c * STEP + u >= beyond
                rows_vmem[r * SLOTS + head + c * STEP + u] = jnp.where(
                    past, zero_rows[0], picked[u]
                )

        for c in range((KEPT - head) // STEP):
            pl.when(c * STEP < beyond)(functools.partial(place, c))
        outs[r].start()
    flat = rows_vmem.reshape(rows_vmem.shape[0] * LANES, HEAD_DIM)
    for r in range(count):
        scores = lax.dot_general(
            query_ref[r],
            flat[pl.ds(r * ROWS, PAD_ROWS)],
            contract_last,
            preferred_element_type=jnp.float32,
        )
        score_vmem[r * group : (r + 1) * group, :] = scores * scale + bias_ref[r]
    scores = score_vmem[...]
    highest = jnp.maximum(jnp.max(scores, axis=-1, keepdims=True), own_score)
    exponentials = jnp.exp(scores - highest)
    own_exp = jnp.exp(own_score - highest)
    denominator = jnp.sum(exponentials, axis=-1, keepdims=True) + own_exp
    probabilities = exponentials / denominator
    own_prob = (own_exp / denominator).astype(jnp.bfloat16).astype(jnp.float32)
    score_vmem[...] = pltpu.roll(probabilities, 1, axis=1)
    for r in range(count):
        moved = score_vmem[r * group : (r + 1) * group, :].astype(jnp.bfloat16)
        combined = jnp.dot(
            moved, flat[pl.ds(r * ROWS, PAD_ROWS)], preferred_element_type=jnp.float32
        )
        attended_vmem[r] = combined + own_prob[
            r * group : (r + 1) * group
        ] * value_ref[r].astype(jnp.float32)
    attended = jnp.concatenate(
        [attended_vmem[:, h, :] for h in range(HEADS_HERE)], axis=1
    ).astype(jnp.bfloat16)
    share = jnp.dot(attended, weight_ref[...], preferred_element_type=jnp.float32).astype(
        jnp.bfloat16
    )
    width = share_ref.shape[2]
    for e in range(share_ref.shape[0]):
        share_ref[e] = share[:, e * width : (e + 1) * width]
    for r in range(count):
        outs[r].wait()


def gather_attend(
    sources, beyond, places, queries, keys, values, bias, out_weight, direct, relayed, peers
):
    count, group = queries.shape[:2]
    width = out_weight.shape[1] // peers
    whole = lambda: pl.BlockSpec(memory_space=pltpu.VMEM)
    hbm = lambda: pl.BlockSpec(memory_space=pltpu.HBM)
    spare = -(-(PAD_ROWS - ROWS) // (8 * LANES)) * 8
    return pl.pallas_call(
        gather_attend_kernel,
        out_shape=(
            pltpu.HBM((count * SLOTS, LANES, HEAD_DIM), jnp.bfloat16),
            jax.ShapeDtypeStruct((peers, count, width), jnp.bfloat16),
        ),
        grid_spec=pltpu.PrefetchScalarGridSpec(
            num_scalar_prefetch=3,
            grid=(),
            in_specs=[whole() for _ in range(7)],
            out_specs=[hbm(), whole()],
            scratch_shapes=[
                pltpu.VMEM((count * SLOTS + spare, LANES, HEAD_DIM), jnp.bfloat16),
                pltpu.VMEM((count * group, PAD_ROWS), jnp.float32),
                pltpu.VMEM((count, group, HEAD_DIM), jnp.float32),
                pltpu.SemaphoreType.DMA((count,)),
            ],
        ),
        compiler_params=pltpu.CompilerParams(vmem_limit_bytes=16 * 1024 * 1024),
        name="gather_attend",
    )(
        sources,
        beyond,
        places,
        queries,
        keys,
        values,
        bias,
        out_weight,
        direct,
        relayed,
    )


def routes(request_order, retained_counts, block_index, blocks, rows_here):
    relays = blocks - rows_here
    shift = relays.bit_length() - 1
    ids = jnp.arange(request_order.shape[0], dtype=jnp.int32)
    line = jnp.arange(blocks, dtype=jnp.int32)
    target_of = jnp.sum(
        jnp.where(request_order[None, :] == ids[:, None], (ids // rows_here)[None, :], 0), axis=1
    ).reshape(blocks, rows_here)
    rows = retained_counts.reshape(blocks, rows_here) + PAGES
    sent = jnp.sum(
        jnp.where(target_of[:, :, None] == line[None, None, :], rows[:, :, None], 0), axis=1
    )
    free = sent == 0
    beyond = jnp.maximum(sent - ROUND_ONE, 0)
    lower = line[None, :] < line[:, None]
    prefix = lambda array: jnp.sum(jnp.where(lower[None], array[:, None, :], 0), axis=2)
    start = prefix(beyond)
    rank = prefix(free.astype(jnp.int32))
    total = jnp.sum(beyond, axis=1)
    until = lambda ordinal, turn: (ordinal - turn + (relays - 1)) >> shift
    above = lambda array: jnp.sum(jnp.where(lower[:, :, None], array[None], 0), axis=1)
    pick = lambda array: jnp.sum(jnp.where(line[None, :] == block_index, array, 0), axis=1)

    loads = jnp.sum(
        jnp.where(
            free[:, :, None],
            until((start + beyond)[:, None, :], rank[:, :, None])
            - until(start[:, None, :], rank[:, :, None]),
            0,
        ),
        axis=0,
    )
    fits = jnp.all(total <= ROUND_ONE * relays) & jnp.all(loads <= ROUND_TWO)

    turn = pick(rank)
    serves = pick(free.astype(jnp.int32)) > 0
    begin = until(start, turn[:, None])
    passed = jnp.where(serves[:, None], until(start + beyond, turn[:, None]) - begin, 0)
    shifted = line[None, :] * ROUND_TWO + above(passed) - begin
    depth = jnp.arange(64, dtype=jnp.int32)
    ordinal = depth[None, :] * relays + turn[:, None]
    inside = (ordinal[:, :, None] >= start[:, None, :]) & (
        ordinal[:, :, None] < (start + beyond)[:, None, :]
    )
    dest = jnp.sum(jnp.where(inside, shifted[:, None, :], 0), axis=2) + depth[None, :]
    limit = blocks * ROUND_TWO
    good = serves[:, None] & (ordinal < total[:, None]) & (depth < ROUND_ONE)[None, :]
    dest = jnp.where(good, jnp.clip(dest, 0, limit - 1), limit)
    held = jnp.where(serves, jnp.clip(until(total, turn), 0, ROUND_ONE), 0)

    mine_start = pick(start)
    mine_beyond = pick(beyond)
    begin = until(mine_start[:, None], rank)
    passed = jnp.where(free, until((mine_start + mine_beyond)[:, None], rank) - begin, 0)
    shifted = line[None, :] * ROUND_TWO + above(passed) - begin
    entry = jnp.arange(128, dtype=jnp.int32)
    ordinal = mine_start[:, None] + entry[None, :]
    chosen = free[:, None, :] & (rank[:, None, :] == (ordinal & (relays - 1))[:, :, None])
    places = jnp.sum(jnp.where(chosen, shifted[:, None, :], 0), axis=2) + (ordinal >> shift)
    places = jnp.where(
        entry[None, :] < mine_beyond[:, None], jnp.clip(places, 0, limit - 1), 0
    )
    return fits, held, dest, mine_beyond, places


def local(
    hidden_in,
    qkv_weight,
    out_weight,
    cache_pool,
    page_table,
    request_order,
    request_lengths,
    retained_counts,
    retained_positions,
    blended_weight,
):
    rows_here = hidden_in.shape[0]
    head_width = qkv_weight.shape[2]
    heads_here = head_width // HEAD_DIM
    blocks = lax.axis_size("blk")
    peers = lax.axis_size("head")
    block_index = lax.axis_index("blk")
    first = block_index * rows_here
    slot_index = jnp.arange(KEPT, dtype=jnp.int32)
    take = lambda array: lax.dynamic_slice_in_dim(array, first, rows_here, 0)

    source_arguments = (
        block_index,
        page_table,
        request_lengths,
        retained_counts,
        request_order,
        retained_positions,
        blended_weight,
        cache_pool,
        blocks,
    )

    def exchange(rows):
        return lax.all_to_all(
            rows.reshape(blocks, -1, HEAD_DIM), "blk", split_axis=0, concat_axis=0, tiled=True
        )

    direct = exchange(spread(*source_arguments)).reshape(-1, LANES, HEAD_DIM)
    fits, held, dest, beyond, places = routes(
        request_order, retained_counts, block_index, blocks, rows_here
    )

    old_ids = take(request_order)
    sources = old_ids // rows_here
    lengths = request_lengths[old_ids]
    counts = retained_counts[old_ids]
    keep = jnp.where(slot_index[None, :] < counts[:, None], retained_positions[old_ids], CAP)
    spots = jnp.arange(CAP, dtype=jnp.int32)
    dropped = (spots[None, :] < lengths[:, None]) & jnp.logical_not(
        jnp.any(keep[:, :, None] == spots[None, None, :], axis=1)
    )
    dropped_weight = jnp.where(dropped, blended_weight[old_ids], 0.0)
    dropped_mass = jnp.log(1.0 + jnp.sum(dropped_weight.reshape(rows_here, PAGES, PAGE), axis=2))
    page_start = jnp.arange(PAGES, dtype=jnp.int32) * PAGE
    bias_slots = jnp.concatenate(
        [
            jnp.where(slot_index[None, :] < counts[:, None], 0.0, NEG),
            jnp.where(page_start[None, :] < lengths[:, None], dropped_mass, NEG),
        ],
        axis=1,
    )
    columns = jnp.arange(ROWS, dtype=jnp.int32) % LANES
    head_rows = jnp.arange(8, dtype=jnp.int32)
    bias = jnp.where(
        columns[None, None, :] == 2 * head_rows[None, :, None],
        jnp.repeat(bias_slots, LANES, axis=1)[:, None, :],
        NEG,
    )
    bias = jnp.pad(bias, ((0, 0), (0, 0), (0, PAD_ROWS - ROWS)), constant_values=NEG)

    gathered = lax.all_gather(hidden_in, "head", axis=1, tiled=True)
    held, dest, beyond, places, sources, bias, fits, gathered = lax.optimization_barrier(
        (held, dest, beyond, places, sources, bias, fits, gathered)
    )
    relayed = exchange(forward_rows(held, dest, direct, blocks)).reshape(-1, LANES, HEAD_DIM)

    normed = layer_norm(gathered.astype(jnp.float32)).astype(jnp.bfloat16)
    project = lambda index: jnp.dot(
        normed, qkv_weight[:, index], preferred_element_type=jnp.float32
    ).reshape(rows_here, heads_here, HEAD_DIM)
    pad_heads = lambda array: jnp.pad(
        array.astype(jnp.bfloat16), ((0, 0), (0, 8 - heads_here), (0, 0))
    )
    queries = pad_heads(rotate(project(0), lengths))
    new_keys = pad_heads(rotate(project(1), lengths))
    new_values = pad_heads(project(2))

    def whole_shape(packed):
        return (
            packed.reshape(rows_here, SLOTS, heads_here, 2, HEAD_DIM)
            .transpose(0, 1, 3, 2, 4)
            .reshape(rows_here, SLOTS, 2, head_width)
        )

    def two_rounds():
        packed, share = gather_attend(
            sources,
            beyond,
            places,
            queries,
            new_keys,
            new_values,
            bias,
            out_weight,
            direct,
            relayed,
            peers,
        )
        return whole_shape(packed), share

    def one_round():
        arrived = exchange(pack(*source_arguments))
        packed, share = attend(
            sources, queries, new_keys, new_values, bias, out_weight, arrived, peers
        )
        return whole_shape(packed), share

    packed_cache, share = lax.cond(fits, two_rounds, one_round)
    parts = lax.all_to_all(share, "head", split_axis=0, concat_axis=0, tiled=True)
    summed = jnp.sum(parts.astype(jnp.float32), axis=0)
    hidden_out = (hidden_in.astype(jnp.float32) + summed).astype(jnp.bfloat16)
    return (hidden_out, packed_cache)


def solution(mesh):
    return jax.shard_map(
        local,
        mesh=mesh,
        in_specs=(
            P("blk", "head"),
            P(None, None, "head"),
            P("head", None),
            P("blk", None, None, "head"),
            P("blk", None),
            P(),
            P(),
            P(),
            P(),
            P(),
        ),
        out_specs=(P("blk", "head"), P("blk", None, None, "head")),
        check_vma=False,
    )
```

```python
import functools

import jax
import jax.numpy as jnp
from jax import lax
from jax.experimental import pallas as pl
from jax.experimental.pallas import tpu as pltpu
from jax.sharding import PartitionSpec as P

HEAD_DIM = 128
PAGE = 64
PAGES = 4
CAP = 256
KEPT = 128
SLOTS = 132
HEADS_HERE = 2
LANES = HEADS_HERE * 2
ROWS = SLOTS * LANES
PAD_ROWS = 640
NEG = -1e30
ROUND_ONE = 54
ROUND_TWO = 34
STEP = 6

epsilon = 1e-05


def layer_norm(hidden):
    average = jnp.mean(hidden, axis=-1, keepdims=True)
    centered = hidden - average
    variance = jnp.mean(centered * centered, axis=-1, keepdims=True)
    return centered * lax.rsqrt(variance + epsilon)


def rotate(vectors, positions):
    half_dim = vectors.shape[-1] // 2
    inverse_freq = 10000.0 ** (-jnp.arange(half_dim, dtype=jnp.float32) / half_dim)
    angles = positions.astype(jnp.float32)[:, None, None] * inverse_freq
    cosine = jnp.cos(angles)
    sine_part = jnp.sin(angles)
    first_half = vectors[..., :half_dim]
    second_half = vectors[..., half_dim:]
    return jnp.concatenate(
        [
            first_half * cosine - second_half * sine_part,
            second_half * cosine + first_half * sine_part,
        ],
        axis=-1,
    )


def pack_kernel(
    block_ref,
    page_hbm,
    length_hbm,
    count_hbm,
    order_hbm,
    keep_hbm,
    weight_hbm,
    cache_rows_hbm,
    cache_flat_hbm,
    send_hbm,
    rows_vmem,
    flat_vmem,
    out_vmem,
    wide_vmem,
    order_vmem,
    keep_vmem,
    weight_vmem,
    spot_vmem,
    page_smem,
    length_smem,
    count_smem,
    spot_smem,
    small_sem,
    load_sem,
    spot_sem,
    out_sem,
):
    count = keep_vmem.shape[0]
    group = 16
    pool_rows = cache_rows_hbm.shape[0]
    first = pl.multiple_of(block_ref[0] * count, count)
    small = [
        pltpu.make_async_copy(source, target, small_sem.at[n])
        for n, (source, target) in enumerate(
            [
                (keep_hbm.at[pl.ds(first, count)], keep_vmem),
                (count_hbm, count_smem),
                (page_hbm, page_smem),
                (order_hbm, order_vmem),
                (length_hbm, length_smem),
                (weight_hbm.at[pl.ds(first, count)], weight_vmem),
            ]
        )
    ]
    for copy in small:
        copy.start()
    load_rows = pltpu.make_async_copy(
        cache_rows_hbm, rows_vmem.at[pl.ds(0, pool_rows)], load_sem.at[0]
    )
    load_flat = pltpu.make_async_copy(cache_flat_hbm, flat_vmem, load_sem.at[1])
    load_rows.start()
    for copy in small:
        copy.wait()
    load_flat.start()

    keep = keep_vmem[...]
    slot_id = lax.broadcasted_iota(jnp.int32, keep.shape, 1)
    row_id = lax.broadcasted_iota(jnp.int32, keep.shape, 0)
    counts = jnp.zeros(keep.shape, jnp.int32)
    base = jnp.zeros(keep.shape, jnp.int32)
    page_of = keep >> 6
    for i in range(count):
        here = row_id == i
        counts = jnp.where(here, count_smem[first + i], counts)
        for j in range(PAGES):
            base = jnp.where(here & (page_of == j), page_smem[j, i] * PAGE, base)
    keep = jnp.where(slot_id < counts, keep, CAP)
    spot_vmem[...] = jnp.where(slot_id < counts, base + (keep & (PAGE - 1)), pool_rows)
    move_spots = pltpu.make_async_copy(spot_vmem, spot_smem, spot_sem)
    move_spots.start()

    order = order_vmem[...]
    place = (
        lax.broadcasted_iota(jnp.int32, order.shape, 0) * order.shape[1]
        + lax.broadcasted_iota(jnp.int32, order.shape, 1)
    ) // count
    targets = [jnp.sum(jnp.where(order == first + i, place, 0)) for i in range(count)]

    keep_cols = jnp.transpose(keep.astype(jnp.float32))
    lane_pos = lax.broadcasted_iota(jnp.int32, (KEPT, CAP), 1).astype(jnp.float32)
    spot = lax.broadcasted_iota(jnp.int32, (1, CAP), 1)
    factors = []
    for i in range(count):
        match = keep_cols[:, i : i + 1] == lane_pos
        kept = jnp.max(jnp.where(match, 1.0, 0.0), axis=0, keepdims=True)
        dropped = (spot < length_smem[first + i]) & (kept < 0.5)
        factors.append(jnp.where(dropped, weight_vmem[i : i + 1, :], 0.0))
    factors = jnp.concatenate(factors, axis=0).astype(jnp.bfloat16)
    spread = (
        lax.broadcasted_iota(jnp.int32, (CAP, CAP * LANES), 1) >> 2
        == lax.broadcasted_iota(jnp.int32, (CAP, CAP * LANES), 0)
    )
    spread = jnp.where(spread, 1.0, 0.0).astype(jnp.bfloat16)
    wide_vmem[...] = jnp.dot(factors, spread, preferred_element_type=jnp.float32)
    page_lanes = PAGE * LANES
    out_row = lax.broadcasted_iota(jnp.int32, (PAGES * LANES, page_lanes), 0)
    out_lane = lax.broadcasted_iota(jnp.int32, (PAGES * LANES, page_lanes), 1)
    same = (out_row & (LANES - 1)) == (out_lane & (LANES - 1))
    selectors = [jnp.where(same & (out_row >> 2 == j), 1.0, 0.0) for j in range(PAGES)]

    zero_rows = jnp.zeros((group, LANES, HEAD_DIM), jnp.bfloat16)
    rows_vmem[pool_rows] = zero_rows[0]

    def clear(c, carry):
        for i in range(count):
            out_vmem[i, pl.ds(pl.multiple_of(c * group, group), group)] = zero_rows
        return carry

    lax.fori_loop(0, KEPT // group, clear, 0)
    move_spots.wait()
    load_rows.wait()
    for i in range(count):

        def gather(c, carry):
            picked = [rows_vmem[spot_smem[i, c * group + u]] for u in range(group)]
            for u in range(group):
                out_vmem[i, c * group + u] = picked[u]
            return carry

        full = (count_smem[first + i] + group - 1) >> 4
        lax.fori_loop(0, full, gather, 0)

    copies = [
        pltpu.make_async_copy(out_vmem.at[i], send_hbm.at[targets[i]], out_sem.at[i])
        for i in range(count)
    ]
    load_flat.wait()
    for i in range(count):
        merged = jnp.zeros((PAGES * LANES, HEAD_DIM), jnp.float32)
        for j in range(PAGES):
            wide = wide_vmem[i : i + 1, j * page_lanes : (j + 1) * page_lanes]
            merged = merged + jnp.dot(
                (selectors[j] * wide).astype(jnp.bfloat16),
                flat_vmem[page_smem[j, i]],
                preferred_element_type=jnp.float32,
            )
        out_vmem[i, pl.ds(KEPT, PAGES)] = merged.astype(jnp.bfloat16).reshape(
            PAGES, LANES, HEAD_DIM
        )
        copies[i].start()
    for copy in copies:
        copy.wait()


def pack(block_index, page_table, lengths, counts, order, positions, weights, cache_pool, blocks):
    count = page_table.shape[0]
    pool = cache_pool.shape[0]
    view = cache_pool.reshape(pool, PAGE, 2, HEADS_HERE, HEAD_DIM).transpose(0, 1, 3, 2, 4)
    as_rows = view.reshape(pool * PAGE, LANES, HEAD_DIM)
    as_flat = view.reshape(pool, PAGE * LANES, HEAD_DIM)
    requests = order.shape[0]
    hbm = lambda: pl.BlockSpec(memory_space=pltpu.HBM)
    operands = [
        page_table.T,
        lengths,
        counts,
        order.reshape(requests // 128, 128),
        positions,
        weights,
        as_rows,
        as_flat,
    ]
    operands = [pltpu.with_memory_space_constraint(x, pltpu.HBM) for x in operands]
    return pl.pallas_call(
        pack_kernel,
        out_shape=pltpu.HBM((blocks, SLOTS, LANES, HEAD_DIM), jnp.bfloat16),
        grid_spec=pltpu.PrefetchScalarGridSpec(
            num_scalar_prefetch=1,
            grid=(),
            in_specs=[hbm() for _ in operands],
            out_specs=hbm(),
            scratch_shapes=[
                pltpu.VMEM((pool * PAGE + 1, LANES, HEAD_DIM), jnp.bfloat16),
                pltpu.VMEM((pool, PAGE * LANES, HEAD_DIM), jnp.bfloat16),
                pltpu.VMEM((count, SLOTS, LANES, HEAD_DIM), jnp.bfloat16),
                pltpu.VMEM((count, CAP * LANES), jnp.float32),
                pltpu.VMEM((requests // 128, 128), jnp.int32),
                pltpu.VMEM((count, KEPT), jnp.int32),
                pltpu.VMEM((count, CAP), jnp.float32),
                pltpu.VMEM((count, KEPT), jnp.int32),
                pltpu.SMEM((PAGES, count), jnp.int32),
                pltpu.SMEM((requests,), jnp.int32),
                pltpu.SMEM((requests,), jnp.int32),
                pltpu.SMEM((count, KEPT), jnp.int32),
                pltpu.SemaphoreType.DMA((6,)),
                pltpu.SemaphoreType.DMA((2,)),
                pltpu.SemaphoreType.DMA(()),
                pltpu.SemaphoreType.DMA((count,)),
            ],
        ),
        compiler_params=pltpu.CompilerParams(vmem_limit_bytes=24 * 1024 * 1024),
        name="pack",
    )(jnp.reshape(block_index, (1,)), *operands)


def attend_kernel(
    source_ref,
    query_ref,
    key_ref,
    value_ref,
    bias_ref,
    weight_ref,
    recv_hbm,
    packed_hbm,
    share_ref,
    rows_vmem,
    score_vmem,
    attended_vmem,
    in_sem,
    out_sem,
):
    count = query_ref.shape[0]
    group = query_ref.shape[1]
    ins = [
        pltpu.make_async_copy(
            recv_hbm.at[source_ref[r]], rows_vmem.at[r, pl.ds(0, ROWS)], in_sem.at[r]
        )
        for r in range(count)
    ]
    outs = [
        pltpu.make_async_copy(rows_vmem.at[r, pl.ds(0, ROWS)], packed_hbm.at[r], out_sem.at[r])
        for r in range(count)
    ]
    for r in range(count):
        ins[r].start()
    for r in range(count):
        rows_vmem[r, pl.ds(ROWS, PAD_ROWS - ROWS)] = jnp.zeros(
            (PAD_ROWS - ROWS, HEAD_DIM), jnp.bfloat16
        )
    scale = HEAD_DIM ** (-0.5)
    contract_last = (((1,), (1,)), ((), ()))
    own_score = (
        jnp.sum(
            query_ref[...].astype(jnp.float32) * key_ref[...].astype(jnp.float32),
            axis=-1,
            keepdims=True,
        )
        * scale
    ).reshape(count * group, 1)
    for r in range(count):
        ins[r].wait()
        outs[r].start()
        scores = lax.dot_general(
            query_ref[r], rows_vmem[r], contract_last, preferred_element_type=jnp.float32
        )
        score_vmem[r * group : (r + 1) * group, :] = scores * scale + bias_ref[r]
    scores = score_vmem[...]
    highest = jnp.maximum(jnp.max(scores, axis=-1, keepdims=True), own_score)
    exponentials = jnp.exp(scores - highest)
    own_exp = jnp.exp(own_score - highest)
    denominator = jnp.sum(exponentials, axis=-1, keepdims=True) + own_exp
    probabilities = exponentials / denominator
    own_prob = (own_exp / denominator).astype(jnp.bfloat16).astype(jnp.float32)
    score_vmem[...] = pltpu.roll(probabilities, 1, axis=1)
    for r in range(count):
        moved = score_vmem[r * group : (r + 1) * group, :].astype(jnp.bfloat16)
        combined = jnp.dot(moved, rows_vmem[r], preferred_element_type=jnp.float32)
        attended_vmem[r] = combined + own_prob[
            r * group : (r + 1) * group
        ] * value_ref[r].astype(jnp.float32)
    attended = jnp.concatenate(
        [attended_vmem[:, h, :] for h in range(HEADS_HERE)], axis=1
    ).astype(jnp.bfloat16)
    share = jnp.dot(attended, weight_ref[...], preferred_element_type=jnp.float32).astype(
        jnp.bfloat16
    )
    width = share_ref.shape[2]
    for e in range(share_ref.shape[0]):
        share_ref[e] = share[:, e * width : (e + 1) * width]
    for r in range(count):
        outs[r].wait()


def attend(sources, queries, keys, values, bias, out_weight, recv, peers):
    count, group = queries.shape[:2]
    width = out_weight.shape[1] // peers
    whole = lambda: pl.BlockSpec(memory_space=pltpu.VMEM)
    hbm = lambda: pl.BlockSpec(memory_space=pltpu.HBM)
    return pl.pallas_call(
        attend_kernel,
        out_shape=(
            pltpu.HBM((count, ROWS, HEAD_DIM), jnp.bfloat16),
            jax.ShapeDtypeStruct((peers, count, width), jnp.bfloat16),
        ),
        grid_spec=pltpu.PrefetchScalarGridSpec(
            num_scalar_prefetch=1,
            grid=(),
            in_specs=[whole(), whole(), whole(), whole(), whole(), hbm()],
            out_specs=[hbm(), whole()],
            scratch_shapes=[
                pltpu.VMEM((count, PAD_ROWS, HEAD_DIM), jnp.bfloat16),
                pltpu.VMEM((count * group, PAD_ROWS), jnp.float32),
                pltpu.VMEM((count, group, HEAD_DIM), jnp.float32),
                pltpu.SemaphoreType.DMA((count,)),
                pltpu.SemaphoreType.DMA((count,)),
            ],
        ),
        compiler_params=pltpu.CompilerParams(vmem_limit_bytes=16 * 1024 * 1024),
        name="attend",
    )(sources, queries, keys, values, bias, out_weight, recv)


def spread_kernel(
    block_ref,
    page_hbm,
    length_hbm,
    count_hbm,
    order_hbm,
    keep_hbm,
    weight_hbm,
    cache_rows_hbm,
    send_hbm,
    rows_vmem,
    out_vmem,
    wide_vmem,
    order_vmem,
    keep_vmem,
    weight_vmem,
    spot_vmem,
    dest_vmem,
    page_smem,
    length_smem,
    count_smem,
    spot_smem,
    dest_smem,
    used_smem,
    free_smem,
    small_sem,
    load_sem,
    spot_sem,
    dest_sem,
    out_sem,
):
    count = keep_vmem.shape[0]
    group = 16
    pool_rows = cache_rows_hbm.shape[0]
    slots = send_hbm.shape[0] // ROUND_ONE
    relays = slots - count
    shift = relays.bit_length() - 1
    first = pl.multiple_of(block_ref[0] * count, count)
    small = [
        pltpu.make_async_copy(source, target, small_sem.at[n])
        for n, (source, target) in enumerate(
            [
                (keep_hbm.at[pl.ds(first, count)], keep_vmem),
                (count_hbm, count_smem),
                (page_hbm, page_smem),
                (order_hbm, order_vmem),
                (length_hbm, length_smem),
                (weight_hbm.at[pl.ds(first, count)], weight_vmem),
            ]
        )
    ]
    for copy in small:
        copy.start()
    load_rows = pltpu.make_async_copy(
        cache_rows_hbm, rows_vmem.at[pl.ds(0, pool_rows)], load_sem
    )
    load_rows.start()
    for copy in small:
        copy.wait()

    order = order_vmem[...]
    place = (
        lax.broadcasted_iota(jnp.int32, order.shape, 0) * order.shape[1]
        + lax.broadcasted_iota(jnp.int32, order.shape, 1)
    ) // count
    targets = [jnp.sum(jnp.where(order == first + i, place, 0)) for i in range(count)]

    keep = keep_vmem[...]
    slot_id = lax.broadcasted_iota(jnp.int32, keep.shape, 1)
    row_id = lax.broadcasted_iota(jnp.int32, keep.shape, 0)
    counts = jnp.zeros(keep.shape, jnp.int32)
    base = jnp.zeros(keep.shape, jnp.int32)
    target = jnp.zeros(keep.shape, jnp.int32)
    page_of = keep >> 6
    for i in range(count):
        here = row_id == i
        counts = jnp.where(here, count_smem[first + i], counts)
        target = jnp.where(here, targets[i], target)
        for j in range(PAGES):
            base = jnp.where(here & (page_of == j), page_smem[j, i] * PAGE, base)
    keep = jnp.where(slot_id < counts, keep, CAP)
    spot_vmem[...] = jnp.where(slot_id < counts, base + (keep & (PAGE - 1)), pool_rows)
    move_spots = pltpu.make_async_copy(spot_vmem, spot_smem, spot_sem)
    move_spots.start()

    for m in range(slots):
        used_smem[m] = 0
    for i in range(count):
        used_smem[targets[i]] = 1
    free = 0
    for m in range(slots):
        free_smem[free] = m
        free = free + 1 - used_smem[m]
    before = jnp.zeros(keep.shape, jnp.int32)
    for i in range(count):
        beyond = jnp.maximum(count_smem[first + i] + PAGES - ROUND_ONE, 0)
        before = before + jnp.where(target > targets[i], beyond, 0)
    entry = slot_id + PAGES
    ordinal = jnp.maximum(before + entry - ROUND_ONE, 0)
    turn = ordinal & (relays - 1)
    relay = jnp.zeros(keep.shape, jnp.int32)
    for j in range(relays):
        relay = jnp.where(turn == j, free_smem[j], relay)
    depth = jnp.minimum(ordinal >> shift, ROUND_ONE - 1)
    dest = jnp.where(
        entry < ROUND_ONE, target * ROUND_ONE + entry, relay * ROUND_ONE + depth
    )
    dest_vmem[...] = jnp.where(slot_id < counts, dest, slots * ROUND_ONE)
    move_dests = pltpu.make_async_copy(dest_vmem, dest_smem, dest_sem)
    move_dests.start()

    keep_cols = jnp.transpose(keep.astype(jnp.float32))
    lane_pos = lax.broadcasted_iota(jnp.int32, (KEPT, CAP), 1).astype(jnp.float32)
    spot = lax.broadcasted_iota(jnp.int32, (1, CAP), 1)
    factors = []
    for i in range(count):
        match = keep_cols[:, i : i + 1] == lane_pos
        kept = jnp.max(jnp.where(match, 1.0, 0.0), axis=0, keepdims=True)
        dropped = (spot < length_smem[first + i]) & (kept < 0.5)
        factors.append(jnp.where(dropped, weight_vmem[i : i + 1, :], 0.0))
    factors = jnp.concatenate(factors, axis=0).astype(jnp.bfloat16)
    repeat = (
        lax.broadcasted_iota(jnp.int32, (CAP, CAP * LANES), 1) >> 2
        == lax.broadcasted_iota(jnp.int32, (CAP, CAP * LANES), 0)
    )
    repeat = jnp.where(repeat, 1.0, 0.0).astype(jnp.bfloat16)
    wide_vmem[...] = jnp.dot(factors, repeat, preferred_element_type=jnp.float32)
    page_lanes = PAGE * LANES
    out_row = lax.broadcasted_iota(jnp.int32, (PAGES * LANES, page_lanes), 0)
    out_lane = lax.broadcasted_iota(jnp.int32, (PAGES * LANES, page_lanes), 1)
    same = (out_row & (LANES - 1)) == (out_lane & (LANES - 1))
    selectors = [jnp.where(same & (out_row >> 2 == j), 1.0, 0.0) for j in range(PAGES)]

    zero_rows = jnp.zeros((group, LANES, HEAD_DIM), jnp.bfloat16)
    rows_vmem[pl.ds(pool_rows, 8)] = zero_rows[:8]

    def clear(c, carry):
        for u in range(4):
            out_vmem[pl.ds(pl.multiple_of((c * 4 + u) * group, group), group)] = zero_rows
        return carry

    lax.fori_loop(0, slots * ROUND_ONE // (4 * group), clear, 0)
    move_spots.wait()
    move_dests.wait()
    load_rows.wait()
    straight = (ROUND_ONE - PAGES) // group
    for i in range(count):
        slot = targets[i] * ROUND_ONE + PAGES
        full = (count_smem[first + i] + group - 1) >> 4

        def gather(c):
            picked = [rows_vmem[spot_smem[i, c * group + u]] for u in range(group)]
            for u in range(group):
                out_vmem[slot + c * group + u] = picked[u]

        def scatter(c):
            picked = [rows_vmem[spot_smem[i, c * group + u]] for u in range(group)]
            for u in range(group):
                out_vmem[dest_smem[i, c * group + u]] = picked[u]

        for c in range(straight):
            gather(c)
        for c in range(straight, KEPT // group):
            pl.when(c < full)(functools.partial(scatter, c))

    flat = rows_vmem.reshape(rows_vmem.shape[0] * LANES, HEAD_DIM)
    for i in range(count):
        merged = jnp.zeros((PAGES * LANES, HEAD_DIM), jnp.float32)
        for j in range(PAGES):
            wide = wide_vmem[i : i + 1, j * page_lanes : (j + 1) * page_lanes]
            start = pl.multiple_of(page_smem[j, i] * page_lanes, page_lanes)
            merged = merged + jnp.dot(
                (selectors[j] * wide).astype(jnp.bfloat16),
                flat[pl.ds(start, page_lanes)],
                preferred_element_type=jnp.float32,
            )
        out_vmem[pl.ds(targets[i] * ROUND_ONE, PAGES)] = merged.astype(jnp.bfloat16).reshape(
            PAGES, LANES, HEAD_DIM
        )
    out = pltpu.make_async_copy(out_vmem.at[pl.ds(0, slots * ROUND_ONE)], send_hbm, out_sem)
    out.start()
    out.wait()


def spread(block_index, page_table, lengths, counts, order, positions, weights, cache_pool, blocks):
    count = page_table.shape[0]
    pool = cache_pool.shape[0]
    view = cache_pool.reshape(pool, PAGE, 2, HEADS_HERE, HEAD_DIM).transpose(0, 1, 3, 2, 4)
    as_rows = view.reshape(pool * PAGE, LANES, HEAD_DIM)
    requests = order.shape[0]
    hbm = lambda: pl.BlockSpec(memory_space=pltpu.HBM)
    operands = [
        page_table.T,
        lengths,
        counts,
        order.reshape(requests // 128, 128),
        positions,
        weights,
        as_rows,
    ]
    operands = [pltpu.with_memory_space_constraint(x, pltpu.HBM) for x in operands]
    return pl.pallas_call(
        spread_kernel,
        out_shape=pltpu.HBM((blocks * ROUND_ONE, LANES, HEAD_DIM), jnp.bfloat16),
        grid_spec=pltpu.PrefetchScalarGridSpec(
            num_scalar_prefetch=1,
            grid=(),
            in_specs=[hbm() for _ in operands],
            out_specs=hbm(),
            scratch_shapes=[
                pltpu.VMEM((pool * PAGE + 8, LANES, HEAD_DIM), jnp.bfloat16),
                pltpu.VMEM((blocks * ROUND_ONE + 8, LANES, HEAD_DIM), jnp.bfloat16),
                pltpu.VMEM((count, CAP * LANES), jnp.float32),
                pltpu.VMEM((requests // 128, 128), jnp.int32),
                pltpu.VMEM((count, KEPT), jnp.int32),
                pltpu.VMEM((count, CAP), jnp.float32),
                pltpu.VMEM((count, KEPT), jnp.int32),
                pltpu.VMEM((count, KEPT), jnp.int32),
                pltpu.SMEM((PAGES, count), jnp.int32),
                pltpu.SMEM((requests,), jnp.int32),
                pltpu.SMEM((requests,), jnp.int32),
                pltpu.SMEM((count, KEPT), jnp.int32),
                pltpu.SMEM((count, KEPT), jnp.int32),
                pltpu.SMEM((blocks,), jnp.int32),
                pltpu.SMEM((blocks + 1,), jnp.int32),
                pltpu.SemaphoreType.DMA((6,)),
                pltpu.SemaphoreType.DMA(()),
                pltpu.SemaphoreType.DMA(()),
                pltpu.SemaphoreType.DMA(()),
                pltpu.SemaphoreType.DMA(()),
            ],
        ),
        compiler_params=pltpu.CompilerParams(vmem_limit_bytes=20 * 1024 * 1024),
        name="spread",
    )(jnp.reshape(block_index, (1,)), *operands)


def relay_kernel(held_ref, dest_ref, recv_ref, send_hbm, out_vmem, out_sem):
    slots = held_ref.shape[0]

    for s in range(slots):
        held = held_ref[s]

        def forward(c):
            start = s * ROUND_ONE + c * STEP
            picked = [recv_ref[start + u] for u in range(STEP)]
            for u in range(STEP):
                out_vmem[dest_ref[s, c * STEP + u]] = picked[u]

        @pl.when(held > 0)
        def _():
            for c in range(3):
                forward(c)
            for c in range(3, ROUND_ONE // STEP):
                pl.when(c * STEP < held)(functools.partial(forward, c))

    out = pltpu.make_async_copy(out_vmem.at[pl.ds(0, slots * ROUND_TWO)], send_hbm, out_sem)
    out.start()
    out.wait()


def forward_rows(held, dest, recv, blocks):
    return pl.pallas_call(
        relay_kernel,
        out_shape=pltpu.HBM((blocks * ROUND_TWO, LANES, HEAD_DIM), jnp.bfloat16),
        grid_spec=pltpu.PrefetchScalarGridSpec(
            num_scalar_prefetch=2,
            grid=(),
            in_specs=[pl.BlockSpec(memory_space=pltpu.VMEM)],
            out_specs=pl.BlockSpec(memory_space=pltpu.HBM),
            scratch_shapes=[
                pltpu.VMEM((blocks * ROUND_TWO + 8, LANES, HEAD_DIM), jnp.bfloat16),
                pltpu.SemaphoreType.DMA(()),
            ],
        ),
        compiler_params=pltpu.CompilerParams(vmem_limit_bytes=12 * 1024 * 1024),
        name="relay",
    )(held, dest, recv)


def gather_attend_kernel(
    source_ref,
    beyond_ref,
    place_ref,
    query_ref,
    key_ref,
    value_ref,
    bias_ref,
    weight_ref,
    direct_ref,
    relayed_ref,
    packed_hbm,
    share_ref,
    rows_vmem,
    score_vmem,
    attended_vmem,
    out_sem,
):
    count, group = query_ref.shape[:2]
    head = ROUND_ONE - PAGES
    zero_rows = jnp.zeros((8, LANES, HEAD_DIM), jnp.bfloat16)
    for r in range(count):
        for c in range(head, KEPT, 8):
            rows_vmem[pl.ds(r * SLOTS + min(c, KEPT - 8), 8)] = zero_rows
    for c in range((rows_vmem.shape[0] - count * SLOTS) // 8):
        rows_vmem[pl.ds(count * SLOTS + c * 8, 8)] = zero_rows
    scale = HEAD_DIM ** (-0.5)
    contract_last = (((1,), (1,)), ((), ()))
    own_score = (
        jnp.sum(
            query_ref[...].astype(jnp.float32) * key_ref[...].astype(jnp.float32),
            axis=-1,
            keepdims=True,
        )
        * scale
    ).reshape(count * group, 1)
    outs = [
        pltpu.make_async_copy(
            rows_vmem.at[pl.ds(r * SLOTS, SLOTS)],
            packed_hbm.at[pl.ds(r * SLOTS, SLOTS)],
            out_sem.at[r],
        )
        for r in range(count)
    ]
    for r in range(count):
        source = source_ref[r]
        beyond = beyond_ref[source]
        start = source * ROUND_ONE
        rows_vmem[pl.ds(r * SLOTS, head)] = direct_ref[pl.ds(start + PAGES, head)]
        rows_vmem[pl.ds(r * SLOTS + KEPT, PAGES)] = direct_ref[pl.ds(start, PAGES)]

        def place(c):
            picked = [relayed_ref[place_ref[source, c * STEP + u]] for u in range(STEP)]
            for u in range(STEP):
                past = c * STEP + u >= beyond
                rows_vmem[r * SLOTS + head + c * STEP + u] = jnp.where(
                    past, zero_rows[0], picked[u]
                )

        for c in range((KEPT - head) // STEP):
            pl.when(c * STEP < beyond)(functools.partial(place, c))
        outs[r].start()
    flat = rows_vmem.reshape(rows_vmem.shape[0] * LANES, HEAD_DIM)
    for r in range(count):
        scores = lax.dot_general(
            query_ref[r],
            flat[pl.ds(r * ROWS, PAD_ROWS)],
            contract_last,
            preferred_element_type=jnp.float32,
        )
        score_vmem[r * group : (r + 1) * group, :] = scores * scale + bias_ref[r]
    scores = score_vmem[...]
    highest = jnp.maximum(jnp.max(scores, axis=-1, keepdims=True), own_score)
    exponentials = jnp.exp(scores - highest)
    own_exp = jnp.exp(own_score - highest)
    denominator = jnp.sum(exponentials, axis=-1, keepdims=True) + own_exp
    probabilities = exponentials / denominator
    own_prob = (own_exp / denominator).astype(jnp.bfloat16).astype(jnp.float32)
    score_vmem[...] = pltpu.roll(probabilities, 1, axis=1)
    for r in range(count):
        moved = score_vmem[r * group : (r + 1) * group, :].astype(jnp.bfloat16)
        combined = jnp.dot(
            moved, flat[pl.ds(r * ROWS, PAD_ROWS)], preferred_element_type=jnp.float32
        )
        attended_vmem[r] = combined + own_prob[
            r * group : (r + 1) * group
        ] * value_ref[r].astype(jnp.float32)
    attended = jnp.concatenate(
        [attended_vmem[:, h, :] for h in range(HEADS_HERE)], axis=1
    ).astype(jnp.bfloat16)
    share = jnp.dot(attended, weight_ref[...], preferred_element_type=jnp.float32).astype(
        jnp.bfloat16
    )
    width = share_ref.shape[2]
    for e in range(share_ref.shape[0]):
        share_ref[e] = share[:, e * width : (e + 1) * width]
    for r in range(count):
        outs[r].wait()


def gather_attend(
    sources, beyond, places, queries, keys, values, bias, out_weight, direct, relayed, peers
):
    count, group = queries.shape[:2]
    width = out_weight.shape[1] // peers
    whole = lambda: pl.BlockSpec(memory_space=pltpu.VMEM)
    hbm = lambda: pl.BlockSpec(memory_space=pltpu.HBM)
    spare = -(-(PAD_ROWS - ROWS) // (8 * LANES)) * 8
    return pl.pallas_call(
        gather_attend_kernel,
        out_shape=(
            pltpu.HBM((count * SLOTS, LANES, HEAD_DIM), jnp.bfloat16),
            jax.ShapeDtypeStruct((peers, count, width), jnp.bfloat16),
        ),
        grid_spec=pltpu.PrefetchScalarGridSpec(
            num_scalar_prefetch=3,
            grid=(),
            in_specs=[whole() for _ in range(7)],
            out_specs=[hbm(), whole()],
            scratch_shapes=[
                pltpu.VMEM((count * SLOTS + spare, LANES, HEAD_DIM), jnp.bfloat16),
                pltpu.VMEM((count * group, PAD_ROWS), jnp.float32),
                pltpu.VMEM((count, group, HEAD_DIM), jnp.float32),
                pltpu.SemaphoreType.DMA((count,)),
            ],
        ),
        compiler_params=pltpu.CompilerParams(vmem_limit_bytes=16 * 1024 * 1024),
        name="gather_attend",
    )(
        sources,
        beyond,
        places,
        queries,
        keys,
        values,
        bias,
        out_weight,
        direct,
        relayed,
    )


def routes(request_order, retained_counts, block_index, blocks, rows_here):
    relays = blocks - rows_here
    shift = relays.bit_length() - 1
    ids = jnp.arange(request_order.shape[0], dtype=jnp.int32)
    line = jnp.arange(blocks, dtype=jnp.int32)
    target_of = jnp.sum(
        jnp.where(request_order[None, :] == ids[:, None], (ids // rows_here)[None, :], 0), axis=1
    ).reshape(blocks, rows_here)
    rows = retained_counts.reshape(blocks, rows_here) + PAGES
    sent = jnp.sum(
        jnp.where(target_of[:, :, None] == line[None, None, :], rows[:, :, None], 0), axis=1
    )
    free = sent == 0
    beyond = jnp.maximum(sent - ROUND_ONE, 0)
    lower = line[None, :] < line[:, None]
    prefix = lambda array: jnp.sum(jnp.where(lower[None], array[:, None, :], 0), axis=2)
    start = prefix(beyond)
    rank = prefix(free.astype(jnp.int32))
    total = jnp.sum(beyond, axis=1)
    until = lambda ordinal, turn: (ordinal - turn + (relays - 1)) >> shift
    above = lambda array: jnp.sum(jnp.where(lower[:, :, None], array[None], 0), axis=1)
    pick = lambda array: jnp.sum(jnp.where(line[None, :] == block_index, array, 0), axis=1)

    loads = jnp.sum(
        jnp.where(
            free[:, :, None],
            until((start + beyond)[:, None, :], rank[:, :, None])
            - until(start[:, None, :], rank[:, :, None]),
            0,
        ),
        axis=0,
    )
    fits = jnp.all(total <= ROUND_ONE * relays) & jnp.all(loads <= ROUND_TWO)

    turn = pick(rank)
    serves = pick(free.astype(jnp.int32)) > 0
    begin = until(start, turn[:, None])
    passed = jnp.where(serves[:, None], until(start + beyond, turn[:, None]) - begin, 0)
    shifted = line[None, :] * ROUND_TWO + above(passed) - begin
    depth = jnp.arange(64, dtype=jnp.int32)
    ordinal = depth[None, :] * relays + turn[:, None]
    inside = (ordinal[:, :, None] >= start[:, None, :]) & (
        ordinal[:, :, None] < (start + beyond)[:, None, :]
    )
    dest = jnp.sum(jnp.where(inside, shifted[:, None, :], 0), axis=2) + depth[None, :]
    limit = blocks * ROUND_TWO
    good = serves[:, None] & (ordinal < total[:, None]) & (depth < ROUND_ONE)[None, :]
    dest = jnp.where(good, jnp.clip(dest, 0, limit - 1), limit)
    held = jnp.where(serves, jnp.clip(until(total, turn), 0, ROUND_ONE), 0)

    mine_start = pick(start)
    mine_beyond = pick(beyond)
    begin = until(mine_start[:, None], rank)
    passed = jnp.where(free, until((mine_start + mine_beyond)[:, None], rank) - begin, 0)
    shifted = line[None, :] * ROUND_TWO + above(passed) - begin
    entry = jnp.arange(128, dtype=jnp.int32)
    ordinal = mine_start[:, None] + entry[None, :]
    chosen = free[:, None, :] & (rank[:, None, :] == (ordinal & (relays - 1))[:, :, None])
    places = jnp.sum(jnp.where(chosen, shifted[:, None, :], 0), axis=2) + (ordinal >> shift)
    places = jnp.where(
        entry[None, :] < mine_beyond[:, None], jnp.clip(places, 0, limit - 1), 0
    )
    return fits, held, dest, mine_beyond, places


def local(
    hidden_in,
    qkv_weight,
    out_weight,
    cache_pool,
    page_table,
    request_order,
    request_lengths,
    retained_counts,
    retained_positions,
    blended_weight,
):
    rows_here = hidden_in.shape[0]
    head_width = qkv_weight.shape[2]
    heads_here = head_width // HEAD_DIM
    blocks = lax.axis_size("blk")
    peers = lax.axis_size("head")
    block_index = lax.axis_index("blk")
    first = block_index * rows_here
    slot_index = jnp.arange(KEPT, dtype=jnp.int32)
    take = lambda array: lax.dynamic_slice_in_dim(array, first, rows_here, 0)

    source_arguments = (
        block_index,
        page_table,
        request_lengths,
        retained_counts,
        request_order,
        retained_positions,
        blended_weight,
        cache_pool,
        blocks,
    )

    def exchange(rows):
        return lax.all_to_all(
            rows.reshape(blocks, -1, HEAD_DIM), "blk", split_axis=0, concat_axis=0, tiled=True
        )

    direct = exchange(spread(*source_arguments)).reshape(-1, LANES, HEAD_DIM)
    fits, held, dest, beyond, places = routes(
        request_order, retained_counts, block_index, blocks, rows_here
    )

    old_ids = take(request_order)
    sources = old_ids // rows_here
    lengths = request_lengths[old_ids]
    counts = retained_counts[old_ids]
    keep = jnp.where(slot_index[None, :] < counts[:, None], retained_positions[old_ids], CAP)
    spots = jnp.arange(CAP, dtype=jnp.int32)
    dropped = (spots[None, :] < lengths[:, None]) & jnp.logical_not(
        jnp.any(keep[:, :, None] == spots[None, None, :], axis=1)
    )
    dropped_weight = jnp.where(dropped, blended_weight[old_ids], 0.0)
    dropped_mass = jnp.log(1.0 + jnp.sum(dropped_weight.reshape(rows_here, PAGES, PAGE), axis=2))
    page_start = jnp.arange(PAGES, dtype=jnp.int32) * PAGE
    bias_slots = jnp.concatenate(
        [
            jnp.where(slot_index[None, :] < counts[:, None], 0.0, NEG),
            jnp.where(page_start[None, :] < lengths[:, None], dropped_mass, NEG),
        ],
        axis=1,
    )
    columns = jnp.arange(ROWS, dtype=jnp.int32) % LANES
    head_rows = jnp.arange(8, dtype=jnp.int32)
    bias = jnp.where(
        columns[None, None, :] == 2 * head_rows[None, :, None],
        jnp.repeat(bias_slots, LANES, axis=1)[:, None, :],
        NEG,
    )
    bias = jnp.pad(bias, ((0, 0), (0, 0), (0, PAD_ROWS - ROWS)), constant_values=NEG)

    gathered = lax.all_gather(hidden_in, "head", axis=1, tiled=True)
    held, dest, beyond, places, sources, bias, fits, gathered = lax.optimization_barrier(
        (held, dest, beyond, places, sources, bias, fits, gathered)
    )
    relayed = exchange(forward_rows(held, dest, direct, blocks)).reshape(-1, LANES, HEAD_DIM)

    normed = layer_norm(gathered.astype(jnp.float32)).astype(jnp.bfloat16)
    project = lambda index: jnp.dot(
        normed, qkv_weight[:, index], preferred_element_type=jnp.float32
    ).reshape(rows_here, heads_here, HEAD_DIM)
    pad_heads = lambda array: jnp.pad(
        array.astype(jnp.bfloat16), ((0, 0), (0, 8 - heads_here), (0, 0))
    )
    queries = pad_heads(rotate(project(0), lengths))
    new_keys = pad_heads(rotate(project(1), lengths))
    new_values = pad_heads(project(2))

    def whole_shape(packed):
        return (
            packed.reshape(rows_here, SLOTS, heads_here, 2, HEAD_DIM)
            .transpose(0, 1, 3, 2, 4)
            .reshape(rows_here, SLOTS, 2, head_width)
        )

    def two_rounds():
        packed, share = gather_attend(
            sources,
            beyond,
            places,
            queries,
            new_keys,
            new_values,
            bias,
            out_weight,
            direct,
            relayed,
            peers,
        )
        return whole_shape(packed), share

    def one_round():
        arrived = exchange(pack(*source_arguments))
        packed, share = attend(
            sources, queries, new_keys, new_values, bias, out_weight, arrived, peers
        )
        return whole_shape(packed), share

    packed_cache, share = lax.cond(fits, two_rounds, one_round)
    parts = lax.all_to_all(share, "head", split_axis=0, concat_axis=0, tiled=True)
    summed = jnp.sum(parts.astype(jnp.float32), axis=0)
    hidden_out = (hidden_in.astype(jnp.float32) + summed).astype(jnp.bfloat16)
    return (hidden_out, packed_cache)


def solution(mesh):
    return jax.shard_map(
        local,
        mesh=mesh,
        in_specs=(
            P("blk", "head"),
            P(None, None, "head"),
            P("head", None),
            P("blk", None, None, "head"),
            P("blk", None),
            P(),
            P(),
            P(),
            P(),
            P(),
        ),
        out_specs=(P("blk", "head"), P("blk", None, None, "head")),
        check_vma=False,
    )
```
